32 devices in a mesh: tm: 4 (over z), space: 8 (over y, x, core).
Axes of the slice: x: 2, y: 2, z: 4, core: 2. Of those that a mesh axis runs over, the one named last changes fastest.
Arguments:
- positions: float32 [3, 8192], P(None, 'space'), may hold values from -6 to 6
- strengths: float32 [3, 8192], P(None, 'space'), may hold values from -6 to 6
- source_lists: int32 [64, 8], P('space'), may hold values from 0 to 63, as said below
- block_slot: int32 [64], replicated, may hold values from 0 to 63, as said below
Outputs:
- slice_ends: float32 [4, 6, 8192], P('tm', None, 'space')
The draws below stay inside these ranges and needn't reach their ends.
Inputs may be any that keep to these rules, and one draw needn't show every extreme that they name: `source_lists`: the 8 ids of a row are distinct. Logical block g is stored as block block_slot[g], on space device block_slot[g] // 8. Among all entries of the 8 rows of one space device, at most 16 are stored on any one space device, and one space device, the same for all rows, holds exactly 16 of the entries of every space device. `block_slot`: A permutation of the logical block ids.
All inputs are finite; a program needn't handle non-finite values.
Results may differ from the reference program's by a relative error of at most 0.0003.
Values sent between devices are 32-bit elements; how exact they have to be, the bound alone decides.
A program may use at most 64 MiB of HBM per device.

```python
import jax
import jax.numpy as jnp
from jax import lax

BLOCK = 128
BLK_DEV = 8
LIST = 8
ITERS = 2
SLICES = 4
NB = 64
NP = 8192
CAP = 16
N_SPACE = 8


def joint_tables(key):
    base_key = jax.random.fold_in(key, 7013)
    slot_key, hot_key, rest_key = jax.random.split(base_key, 3)
    block_slot = jax.random.permutation(slot_key, NB).astype(jnp.int32)
    logical_of = jnp.argsort(block_slot).astype(jnp.int32)
    hot_owner = jax.random.randint(hot_key, (), 0, N_SPACE).astype(jnp.int32)
    request_count = BLK_DEV * LIST
    owner_pool = jnp.repeat(jnp.arange(N_SPACE, dtype=jnp.int32), CAP)

    def one_device(device_key):
        pick_key, local_key, order_key = jax.random.split(device_key, 3)
        scores = jax.random.permutation(pick_key, N_SPACE * CAP).astype(jnp.int32)
        scores = jnp.where(owner_pool == hot_owner, scores - N_SPACE * CAP, scores)
        chosen = owner_pool[jnp.argsort(scores)[:request_count]]
        owners = jnp.sort(chosen)
        onehot = (owners[:, None] == jnp.arange(N_SPACE, dtype=jnp.int32)[None, :]).astype(jnp.int32)
        counts = jnp.sum(onehot, 0)
        group_starts = jnp.cumsum(counts) - counts
        first_of = jnp.sum(onehot * group_starts[None, :], 1)
        serial = jnp.arange(request_count, dtype=jnp.int32)
        rank_within = (serial - first_of) // BLK_DEV
        list_of = serial % BLK_DEV
        local_perm = jnp.argsort(jax.random.randint(local_key, (BLK_DEV, N_SPACE, BLK_DEV), 0, 2 ** 30), axis=-1).astype(jnp.int32)
        local_index = local_perm[list_of, owners, rank_within]
        logical = logical_of[owners * BLK_DEV + local_index]
        table = logical.reshape(LIST, BLK_DEV).T
        shuffle = jnp.argsort(jax.random.randint(order_key, (BLK_DEV, LIST), 0, 2 ** 30), axis=1)
        return jnp.take_along_axis(table, shuffle, axis=1).astype(jnp.int32)
    device_keys = jax.random.split(rest_key, N_SPACE)
    tables = jax.vmap(one_device)(device_keys)
    return (tables.reshape(NB, LIST).astype(jnp.int32), block_slot)


def draw_source_lists(key, part):
    return joint_tables(key)[0]


def draw_block_slot(key, part):
    return joint_tables(key)[1]


def block_levels(key, extent, shards, low, high):
    gain = 1.0
    for axis_at, shards_of in shards:
        heights = jax.random.uniform(jax.random.fold_in(jax.random.fold_in(key, 6), axis_at), (shards_of,), jnp.float32, low / len(shards), high / len(shards))
        gain = gain * jnp.repeat(jnp.exp(heights), extent[axis_at] // shards_of).reshape((-1,) + (1,) * (len(extent) - 1 - axis_at))
    return gain


def bell_draw(rng, extent, width, most, pieces=(), kind=jnp.bfloat16):
    drawn = width * jax.random.normal(rng, extent, jnp.float32)
    if pieces:
        drawn = drawn * block_levels(rng, extent, pieces, -0.22, 0.18)
    return jnp.clip(drawn, -most, most).astype(kind)


def setup_inputs(seed: int = 0) -> dict:
    keys = jax.random.split(jax.random.key(seed), 5)
    return {
        "positions": bell_draw(keys[0], (3, NP), 1.0, 6.0, ((1, 8),), jnp.float32),
        "strengths": bell_draw(keys[1], (3, NP), 1.0, 6.0, ((1, 8),), jnp.float32),
        "source_lists": draw_source_lists(jax.random.fold_in(keys[4], 71), 0),
        "block_slot": draw_block_slot(jax.random.fold_in(keys[4], 71), 0),
    }


time_step = 0.1
core_square = 0.25
inv_four_pi = 0.07957747154594767

def cross_product(first_vec, second_vec):
    return jnp.stack([first_vec[1] * second_vec[2] - first_vec[2] * second_vec[1], first_vec[2] * second_vec[0] - first_vec[0] * second_vec[2], first_vec[0] * second_vec[1] - first_vec[1] * second_vec[0]], 0)

def interact(target, source):
    separation = target[0:3, None, :] - source[0:3, :, None]
    rho_squared = lax.optimization_barrier(jnp.sum(separation * separation, 0)) + core_square
    inverse = lax.rsqrt(rho_squared)
    kernel_three = inverse * inverse * inverse
    kernel_five = kernel_three * inverse * inverse
    alpha_source = source[3:6, :, None]
    alpha_target = target[3:6, None, :]
    r_cross = cross_product(separation, alpha_source)
    a_cross = cross_product(alpha_target, alpha_source)
    a_dot_r = lax.optimization_barrier(jnp.sum(alpha_target * separation, 0))
    velocity = -inv_four_pi * lax.optimization_barrier(jnp.sum(kernel_three * r_cross, 1))
    stretch = -inv_four_pi * lax.optimization_barrier(jnp.sum(kernel_three * a_cross - 3.0 * kernel_five * a_dot_r * r_cross, 1))
    return jnp.concatenate([velocity, stretch], 0)

def evaluate(state_now, source_lists, block_slot):
    tiled_state = state_now.reshape(6, -1, BLOCK)

    def one_block(block_index):
        physical = block_slot[source_lists[block_index]]
        source = tiled_state[:, physical].reshape(6, -1)
        target = lax.dynamic_index_in_dim(tiled_state, block_index, 1, keepdims=False)
        return interact(target, source)
    rate_blocks = lax.map(one_block, jnp.arange(tiled_state.shape[1], dtype=jnp.int32))
    return jnp.moveaxis(rate_blocks, 0, 1).reshape(6, -1)

def fine_sweep(start_state, rate_zero, source_lists, block_slot):
    half_step = 0.5 * time_step
    node_one = start_state + half_step * rate_zero
    rate_one = evaluate(node_one, source_lists, block_slot)
    node_two = node_one + half_step * rate_one
    rate_two = evaluate(node_two, source_lists, block_slot)
    second_one = start_state + time_step * (5.0 / 24.0 * rate_zero + 1.0 / 3.0 * rate_one - 1.0 / 24.0 * rate_two)
    second_rate = evaluate(second_one, source_lists, block_slot)
    return second_one + half_step * (second_rate - rate_one) + time_step * (-1.0 / 24.0 * rate_zero + 1.0 / 3.0 * rate_one + 5.0 / 24.0 * rate_two)

def reference(positions, strengths, source_lists, block_slot):
    initial = jnp.concatenate([positions, strengths], 0)
    rate_initial = evaluate(initial, source_lists, block_slot)
    start_list = [initial] * SLICES
    rate_list = [rate_initial] * SLICES
    end_list = []
    for iteration in range(ITERS):
        corrections = []
        for slice_index in range(SLICES):
            fine_end = fine_sweep(start_list[slice_index], rate_list[slice_index], source_lists, block_slot)
            corrections.append(fine_end - (start_list[slice_index] + time_step * rate_list[slice_index]))
        current = initial
        new_starts = []
        new_rates = []
        end_list = []
        for slice_index in range(SLICES):
            rate_now = evaluate(current, source_lists, block_slot)
            new_starts.append(current)
            new_rates.append(rate_now)
            end_state = current + time_step * rate_now + corrections[slice_index]
            end_list.append(end_state)
            current = end_state
        start_list = new_starts
        rate_list = new_rates
    return jnp.stack(end_list, 0)
```

```python
import functools

import jax
import jax.numpy as jnp
from jax import lax
from jax.experimental import pallas as pl
from jax.experimental.pallas import tpu as pltpu
from jax.sharding import PartitionSpec as P

BLOCK = 128
SUB = 8
PIECES = 3
TERMS = 32
DEPTH = 32
TOGETHER = 8
AHEAD = 6
MESH = pl.DeviceIdType.MESH

time_step = 0.1
core_square = 0.25
inv_four_pi = 0.07957747154594767


def cross(u, v):
    return [
        u[1] * v[2] - u[2] * v[1],
        u[2] * v[0] - u[0] * v[2],
        u[0] * v[1] - u[1] * v[0],
    ]


def dot3(u, v):
    return u[0] * v[0] + u[1] * v[1] + u[2] * v[2]


def rounded(v):
    return v.astype(jnp.bfloat16).astype(jnp.float32)


def split3(v):
    high = rounded(v)
    rest = v - high
    middle = rounded(rest)
    return high, middle, rounded(rest - middle)


def kernel(
    spaces, slices, blocks, width,
    pos_ref, str_ref, list_ref, slot_ref, out_ref,
    gathered, base, rate, f0, f1, f2, c0, incoming, outgoing,
    rows_a, rows_m, feat, moment, coef, send_sem, recv_sem, pass_sem,
):
    me = lax.axis_index("space")
    g = lax.axis_index("tm")
    h = time_step

    barrier = pltpu.get_barrier_semaphore()

    def greet(d, carry):
        peer = lax.rem(me + d, spaces)
        pl.semaphore_signal(barrier, inc=1, device_id={"space": peer}, device_id_type=MESH)
        return carry

    lax.fori_loop(1, spaces, greet, 0)

    @pl.when(g > 0)
    def _():
        pl.semaphore_signal(barrier, inc=1, device_id={"tm": g - 1}, device_id_type=MESH)

    @pl.when(g < slices - 1)
    def _():
        pl.semaphore_signal(barrier, inc=1, device_id={"tm": g + 1}, device_id_type=MESH)

    for b in range(blocks):
        cols = slice(b * BLOCK, (b + 1) * BLOCK)
        for r in range(3):
            gathered[0, me, r, b : b + 1, :] = pos_ref[r : r + 1, cols]
            gathered[0, me, 3 + r, b : b + 1, :] = str_ref[r : r + 1, cols]

    neighbours = jnp.where(g > 0, 1, 0) + jnp.where(g < slices - 1, 1, 0)
    pl.semaphore_wait(barrier, spaces - 1 + neighbours)

    chips = spaces // 2
    tall = chips // 2
    core = lax.rem(me, 2)
    column = lax.rem(me // 2, 2)
    row = me // 4
    partner = me + 1 - 2 * core

    def twin(d, sign):
        other_column = lax.rem(column + d % 2, 2)
        other_row = lax.rem(row + tall + sign * (d // 2), tall)
        return 2 * (2 * other_row + other_column) + core

    def copy(slot, what, where, sem):
        return pltpu.make_async_remote_copy(
            src_ref=gathered.at[slot, what],
            dst_ref=gathered.at[slot, what],
            send_sem=send_sem.at[slot, sem],
            recv_sem=recv_sem.at[slot, what],
            device_id={"space": where},
            device_id_type=MESH,
        )

    order = sorted(range(1, chips), key=lambda d: (-(d % 2) - (d // 2), d))

    def mirror(p):
        return p + 1 - 2 * core

    def sends(slot):
        found = [copy(slot, me, twin(d, 1), d) for d in order]
        found += [copy(slot, me, mirror(twin(d, 1)), chips + d) for d in order]
        return found + [copy(slot, me, partner, 0)]

    def pass_copy():
        return pltpu.make_async_remote_copy(
            src_ref=outgoing,
            dst_ref=incoming,
            send_sem=pass_sem.at[0],
            recv_sem=pass_sem.at[1],
            device_id={"tm": lax.rem(g + 1, slices)},
            device_id_type=MESH,
        )

    def rows_of(ref, values, per):
        for r, v in enumerate(values):
            ref[pl.ds(r, blocks, stride=per), :] = v

    def row_is(*rows):
        at = lax.broadcasted_iota(jnp.int32, (1, SUB, BLOCK), 1)
        found = at == rows[0]
        for r in rows[1:]:
            found = found | (at == r)
        return found

    def source_features(slot, p):
        x = [gathered[slot, p, r] for r in range(3)]
        a = [gathered[slot, p, 3 + r] for r in range(3)]
        square = dot3(x, x)
        zero = jnp.zeros_like(square)
        rows_of(rows_a, x + [square, zero + 1.0] + x, SUB)
        high, middle, low = split3(rows_a[...].reshape(blocks, SUB, BLOCK))
        second = jnp.where(row_is(0, 1, 2, 4), high, middle)
        third = jnp.where(row_is(4), high, jnp.where(row_is(0, 1, 2), middle, low))
        feat[pl.ds(p * blocks, blocks)] = jnp.concatenate(
            [high, second, third, jnp.zeros_like(high)], 1
        ).astype(jnp.bfloat16)
        six = a + cross(x, a)
        rows_of(
            rows_m,
            six + [v * m for v in x + [square] for m in six] + [zero, zero],
            TERMS,
        )
        pieces = split3(rows_m[...].reshape(blocks, TERMS, BLOCK))
        moment[pl.ds(p * blocks, blocks)] = jnp.concatenate(pieces, 1).astype(jnp.bfloat16)

    def target_features(slot):
        x = [gathered[slot, me, r] for r in range(3)]
        square = dot3(x, x) + core_square
        minus = [-2.0 * v for v in x]
        one = jnp.zeros_like(square) + 1.0
        rows_of(rows_a, minus + [one, square] + minus, SUB)
        high, middle, low = split3(rows_a[...].reshape(blocks, SUB, BLOCK))
        first = jnp.where(row_is(0, 1, 2, 3, 4), high, middle)
        second = jnp.where(row_is(3, 5, 6, 7), high, jnp.where(row_is(4), middle, low))
        third = jnp.where(row_is(3, 5, 6, 7), high, jnp.where(row_is(4), low, middle))
        pieces = jnp.concatenate([first, second, third, jnp.zeros_like(first)], 1)
        for b in range(blocks):
            coef[b] = pieces[b].T.astype(jnp.bfloat16)

    group = 2 if width % 2 == 0 else 1

    def pair_product(i, j):
        at = [slot_ref[list_ref[i, j + k]] for k in range(group)]
        right = jnp.concatenate([feat[p] for p in at], 1)
        both = lax.dot_general(
            coef[i], right, (((1,), (0,)), ((), ())), preferred_element_type=jnp.float32
        )
        return at, both

    def pair_sums(at, both):
        inverse = lax.rsqrt(both)
        square = inverse * inverse
        weight = (square * square) * inverse
        high = weight.astype(jnp.bfloat16)
        low = (weight - high.astype(jnp.float32)).astype(jnp.bfloat16)
        sums = jnp.concatenate([moment[p] for p in at], 1)
        return lax.dot_general(
            sums, jnp.concatenate([high, low], 0), (((1,), (1,)), ((), ())),
            preferred_element_type=jnp.float32,
        )

    def some_targets(first, count):
        work = [(i, j) for i in range(count) for j in range(0, width, group)]
        waiting = []
        totals = [0.0] * count
        for k in range(len(work) + AHEAD):
            if k < len(work):
                i, j = work[k]
                waiting.append((i, pair_product(first + i, j)))
            if k >= AHEAD:
                i, (at, both) = waiting.pop(0)
                totals[i] += pair_sums(at, both)
                if k - AHEAD == len(work) - 1 or work[k - AHEAD + 1][0] != i:
                    halves = totals[i][:, :BLOCK] + totals[i][:, BLOCK:]
                    whole = halves[2 * TERMS :] + halves[TERMS : 2 * TERMS] + halves[:TERMS]
                    at_rows = pl.ds(pl.multiple_of((first + i) * TERMS, TERMS), TERMS)
                    rows_m[at_rows, :] = whole

    def all_targets():
        per = TOGETHER if blocks % TOGETHER == 0 else 1

        def body(k, carry):
            some_targets(k * per, per)
            return carry

        lax.fori_loop(0, blocks // per, body, 0)

    def evaluate(slot):
        for each in sends(slot):
            each.start()
        target_features(slot)
        source_features(slot, me)

        def arrived(p):
            copy(slot, p, p, 0).wait_recv()

        near = order[::-1]
        arrived(partner)
        source_features(slot, partner)
        for d in near:
            arrived(twin(d, -1))
            source_features(slot, twin(d, -1))
        for d in near:
            arrived(mirror(twin(d, -1)))
            source_features(slot, mirror(twin(d, -1)))
        all_targets()
        x = [gathered[slot, me, r] for r in range(3)]
        a = [gathered[slot, me, 3 + r] for r in range(3)]
        pick = lambda r: rows_m[pl.ds(r, blocks, stride=TERMS), :]
        plain = [pick(c) for c in range(6)]
        along = [[pick(6 * (k + 1) + c) for c in range(6)] for k in range(3)]
        squared = [pick(24 + c) for c in range(6)]
        near = dot3(x, x) + core_square
        turn = dot3(a, x)
        three = [
            near * plain[c] - 2.0 * dot3(x, [along[k][c] for k in range(3)]) + squared[c]
            for c in range(6)
        ]
        five = [
            turn * plain[c] - dot3(a, [along[k][c] for k in range(3)]) for c in range(6)
        ]
        three_a, three_b = three[:3], three[3:]
        five_a, five_b = five[:3], five[3:]
        cross_v = cross(x, three_a)
        cross_s = cross(a, three_a)
        cross_f = cross(x, five_a)
        for r in range(3):
            rate[r] = -inv_four_pi * (cross_v[r] - three_b[r])
            rate[3 + r] = -inv_four_pi * (cross_s[r] - 3.0 * (cross_f[r] - five_b[r]))
        for each in sends(slot):
            each.wait_send()

    def write_out(value):
        for b in range(blocks):
            for r in range(6):
                out_ref[0, r : r + 1, b * BLOCK : (b + 1) * BLOCK] = value[r, b : b + 1, :]

    second = 3 + g
    steps = jnp.where(g == 0, 4, jnp.where(g < slices - 1, g + 8, g + 7))

    def step(s, carry):
        slot = lax.rem(s, 2)
        other = 1 - slot
        evaluate(slot)
        current = gathered[slot, me]
        now = rate[...]
        part = jnp.where(s < 4, s, s - second)

        @pl.when(part == 0)
        def _():
            base[...] = current
            f0[...] = now
            gathered[other, me] = current + (0.5 * h) * now

        @pl.when(part == 1)
        def _():
            f1[...] = now
            gathered[other, me] = current + (0.5 * h) * now

        @pl.when(part == 2)
        def _():
            f2[...] = now
            gathered[other, me] = base[...] + h * (
                5.0 / 24.0 * f0[...] + 1.0 / 3.0 * f1[...] - 1.0 / 24.0 * now
            )

        @pl.when(part == 3)
        def _():
            end = (
                current
                + (0.5 * h) * (now - f1[...])
                + h * (-1.0 / 24.0 * f0[...] + 1.0 / 3.0 * f1[...] + 5.0 / 24.0 * f2[...])
            )
            coarse = base[...] + h * f0[...]
            correction = end - coarse

            @pl.when(s == 3)
            def _():
                c0[...] = correction

            @pl.when((s > 3) & (g > 1))
            def _():
                pass_copy().wait_recv()
                gathered[other, me] = incoming[...] + correction

            @pl.when((s == 3) | (g <= 1))
            def _():
                gathered[other, me] = coarse + correction

            @pl.when((s > 3) | (g == 0))
            def _():
                write_out(gathered[other, me])

        @pl.when(part < 0)
        def _():
            gathered[other, me] = current + h * now + c0[...]

        @pl.when(part == 4)
        def _():
            outgoing[...] = current + h * now
            handed = pass_copy()
            handed.start()
            handed.wait_send()

        return carry

    lax.fori_loop(0, steps, step, 0)


def per_device(spaces, slices, positions, strengths, source_lists, block_slot):
    blocks, width = source_lists.shape
    whole = block_slot.shape[0]
    state = pltpu.VMEM((6, blocks, BLOCK), jnp.float32)
    vmem = pl.BlockSpec(memory_space=pltpu.VMEM)
    smem = pl.BlockSpec(memory_space=pltpu.SMEM)
    return pl.pallas_call(
        functools.partial(kernel, spaces, slices, blocks, width),
        out_shape=jax.ShapeDtypeStruct((1, 6, blocks * BLOCK), jnp.float32),
        in_specs=[vmem, vmem, smem, smem],
        out_specs=vmem,
        scratch_shapes=[
            pltpu.VMEM((2, spaces, 6, blocks, BLOCK), jnp.float32),
            state, state, state, state, state, state, state, state,
            pltpu.VMEM((blocks * SUB, BLOCK), jnp.float32),
            pltpu.VMEM((blocks * TERMS, BLOCK), jnp.float32),
            pltpu.VMEM((whole, DEPTH, BLOCK), jnp.bfloat16),
            pltpu.VMEM((whole, PIECES * TERMS, BLOCK), jnp.bfloat16),
            pltpu.VMEM((blocks, BLOCK, DEPTH), jnp.bfloat16),
            pltpu.SemaphoreType.DMA((2, spaces)),
            pltpu.SemaphoreType.DMA((2, spaces)),
            pltpu.SemaphoreType.DMA((2,)),
        ],
        compiler_params=pltpu.CompilerParams(collective_id=0, has_side_effects=True),
    )(positions, strengths, source_lists, block_slot)


def solution(mesh):
    return jax.shard_map(
        functools.partial(per_device, mesh.shape["space"], mesh.shape["tm"]),
        mesh=mesh,
        in_specs=(P(None, "space"), P(None, "space"), P("space", None), P()),
        out_specs=P("tm", None, "space"),
        check_vma=False,
    )
```

```python
import functools

import jax
import jax.numpy as jnp
from jax import lax
from jax.experimental import pallas as pl
from jax.experimental.pallas import tpu as pltpu
from jax.sharding import PartitionSpec as P

BLOCK = 128
SUB = 8
PIECES = 3
TERMS = 32
DEPTH = 32
AHEAD = 6
MESH = pl.DeviceIdType.MESH

time_step = 0.1
core_square = 0.25
inv_four_pi = 0.07957747154594767


def cross(u, v):
    return [
        u[1] * v[2] - u[2] * v[1],
        u[2] * v[0] - u[0] * v[2],
        u[0] * v[1] - u[1] * v[0],
    ]


def dot3(u, v):
    return u[0] * v[0] + u[1] * v[1] + u[2] * v[2]


def rounded(v):
    return v.astype(jnp.bfloat16).astype(jnp.float32)


def split3(v):
    high = rounded(v)
    rest = v - high
    middle = rounded(rest)
    return high, middle, rounded(rest - middle)


def kernel(
    spaces, slices, blocks, width, halves,
    pos_ref, str_ref, list_ref, slot_ref, out_ref,
    gathered, now_at, base, f0, f1, f2, c0, incoming, outgoing,
    sums, feat, moment, coef, send_sem, recv_sem, pass_sem,
):
    me = lax.axis_index("space")
    g = lax.axis_index("tm")
    h = time_step
    some = blocks // halves

    barrier = pltpu.get_barrier_semaphore()

    def greet(d, carry):
        peer = lax.rem(me + d, spaces)
        pl.semaphore_signal(barrier, inc=1, device_id={"space": peer}, device_id_type=MESH)
        return carry

    lax.fori_loop(1, spaces, greet, 0)

    @pl.when(g > 0)
    def _():
        pl.semaphore_signal(barrier, inc=1, device_id={"tm": g - 1}, device_id_type=MESH)

    @pl.when(g < slices - 1)
    def _():
        pl.semaphore_signal(barrier, inc=1, device_id={"tm": g + 1}, device_id_type=MESH)

    for b in range(blocks):
        cols = slice(b * BLOCK, (b + 1) * BLOCK)
        half, at = divmod(b, some)
        for r in range(3):
            now_at[half, r, at : at + 1, :] = pos_ref[r : r + 1, cols]
            now_at[half, 3 + r, at : at + 1, :] = str_ref[r : r + 1, cols]
            gathered[0, half, me, at, r : r + 1, :] = pos_ref[r : r + 1, cols]
            gathered[0, half, me, at, 3 + r : 4 + r, :] = str_ref[r : r + 1, cols]

    neighbours = jnp.where(g > 0, 1, 0) + jnp.where(g < slices - 1, 1, 0)
    pl.semaphore_wait(barrier, spaces - 1 + neighbours)

    chips = spaces // 2
    tall = chips // 2
    core = lax.rem(me, 2)
    column = lax.rem(me // 2, 2)
    row = me // 4
    partner = me + 1 - 2 * core

    def twin(d, sign):
        other_column = lax.rem(column + d % 2, 2)
        other_row = lax.rem(row + tall + sign * (d // 2), tall)
        return 2 * (2 * other_row + other_column) + core

    def copy(slot, half, what, where, sem):
        return pltpu.make_async_remote_copy(
            src_ref=gathered.at[slot, half, what],
            dst_ref=gathered.at[slot, half, what],
            send_sem=send_sem.at[slot, half, sem],
            recv_sem=recv_sem.at[slot, half, what],
            device_id={"space": where},
            device_id_type=MESH,
        )

    order = sorted(range(1, chips), key=lambda d: (-(d % 2) - (d // 2), d))

    def mirror(p):
        return p + 1 - 2 * core

    def sends(slot, half):
        found = []
        for d in order:
            found.append(copy(slot, half, me, twin(d, 1), d))
            found.append(copy(slot, half, me, mirror(twin(d, 1)), chips + d))
        return found + [copy(slot, half, me, partner, 0)]

    def pass_copy(half):
        return pltpu.make_async_remote_copy(
            src_ref=outgoing.at[half],
            dst_ref=incoming.at[half],
            send_sem=pass_sem.at[0, half],
            recv_sem=pass_sem.at[1, half],
            device_id={"tm": lax.rem(g + 1, slices)},
            device_id_type=MESH,
        )

    at_row = lax.broadcasted_iota(jnp.int32, (SUB, BLOCK), 0)

    def stack(values):
        found = values[0]
        for r, v in enumerate(values[1:]):
            found = jnp.where(at_row > r, v, found)
        return found

    def spread(v):
        return jnp.broadcast_to(v, (SUB, BLOCK))

    def source_block(slot, half, p, b, centre):
        rows = [gathered[slot, half, p, b, r : r + 1, :] for r in range(6)]
        x = [spread(v) - c for v, c in zip(rows[:3], centre)]
        a = [spread(v) for v in rows[3:]]
        square = dot3(x, x)
        six = a + cross(x, a)
        whole = stack([x[0], x[1], x[2], square, jnp.ones_like(square), x[0], x[1], x[2]])
        high, middle, low = split3(whole)
        second = jnp.where((at_row <= 2) | (at_row == 4), high, middle)
        third = jnp.where(at_row == 4, high, jnp.where(at_row <= 2, middle, low))
        at = p * blocks + half * some + b
        feat[at] = jnp.concatenate(
            [high, second, third, jnp.zeros_like(high)], 0
        ).astype(jnp.bfloat16)
        common = stack(six)
        inner = at_row <= 5
        parts = []
        for k in range(3):
            ends = jnp.where(at_row == 6, six[2 * k], six[2 * k + 1])
            parts.append(jnp.where(inner, common * x[k], ends))
        parts.append(common * square)
        pieces = split3(jnp.concatenate(parts, 0))
        moment[at] = jnp.concatenate(pieces, 0).astype(jnp.bfloat16)

    def source_features(slot, half, p, centre):
        for b in range(some):
            source_block(slot, half, p, b, centre)

    def target_features(slot, centre):
        for half in range(halves):
            for b in range(some):
                x = [
                    spread(gathered[slot, half, me, b, r : r + 1, :]) - centre[r]
                    for r in range(3)
                ]
                square = dot3(x, x) + core_square
                minus = [-2.0 * v for v in x]
                high, middle, low = split3(
                    stack(minus + [jnp.ones_like(square), square] + minus)
                )
                first = jnp.where(at_row <= 4, high, middle)
                exact = (at_row == 3) | (at_row >= 5)
                second = jnp.where(exact, high, jnp.where(at_row == 4, middle, low))
                third = jnp.where(exact, high, jnp.where(at_row == 4, low, middle))
                pieces = jnp.concatenate([first, second, third, jnp.zeros_like(first)], 0)
                coef[half * some + b] = pieces.T.astype(jnp.bfloat16)

    group = 2 if width % 2 == 0 else 1

    def pair_product(i, j):
        at = [slot_ref[list_ref[i, j + k]] for k in range(group)]
        right = jnp.concatenate([feat[p] for p in at], 1)
        both = lax.dot_general(
            coef[i], right, (((1,), (0,)), ((), ())), preferred_element_type=jnp.float32
        )
        return at, both

    def pair_sums(at, both):
        inverse = lax.rsqrt(both)
        square = inverse * inverse
        weight = (square * square) * inverse
        high = weight.astype(jnp.bfloat16)
        low = (weight - high.astype(jnp.float32)).astype(jnp.bfloat16)
        moments = jnp.concatenate([moment[p] for p in at], 1)
        return lax.dot_general(
            moments, jnp.concatenate([high, low], 0), (((1,), (1,)), ((), ())),
            preferred_element_type=jnp.float32,
        )

    def all_targets(finish):
        work = [(i, j) for i in range(blocks) for j in range(0, width, group)]
        waiting = []
        total = 0.0
        for k in range(len(work) + AHEAD):
            if k < len(work):
                i, j = work[k]
                waiting.append((i, pair_product(i, j)))
            if k >= AHEAD:
                i, (at, both) = waiting.pop(0)
                total += pair_sums(at, both)
                if k - AHEAD == len(work) - 1 or work[k - AHEAD + 1][0] != i:
                    joined = total[:, :BLOCK] + total[:, BLOCK:]
                    sums[i * TERMS : (i + 1) * TERMS, :] = (
                        joined[2 * TERMS :] + joined[TERMS : 2 * TERMS] + joined[:TERMS]
                    )
                    total = 0.0
                    if (i + 1) % some == 0:
                        finish(i // some)

    def rates(half, centre):
        x = [now_at[half, r] - centre[r] for r in range(3)]
        a = [now_at[half, 3 + r] for r in range(3)]
        pick = lambda r: sums[pl.ds(half * some * TERMS + r, some, stride=TERMS), :]
        plain = [pick(SUB * (c // 2) + 6 + c % 2) for c in range(6)]
        along = [[pick(SUB * k + c) for c in range(6)] for k in range(3)]
        squared = [pick(SUB * 3 + c) for c in range(6)]
        near = dot3(x, x) + core_square
        turn = dot3(a, x)
        three = [
            near * plain[c] - 2.0 * dot3(x, [along[k][c] for k in range(3)]) + squared[c]
            for c in range(6)
        ]
        five = [
            turn * plain[c] - dot3(a, [along[k][c] for k in range(3)]) for c in range(6)
        ]
        cross_v = cross(x, three[:3])
        cross_s = cross(a, three[:3])
        cross_f = cross(x, five[:3])
        velocity = [-inv_four_pi * (cross_v[r] - three[3 + r]) for r in range(3)]
        stretch = [
            -inv_four_pi * (cross_s[r] - 3.0 * (cross_f[r] - five[3 + r])) for r in range(3)
        ]
        return velocity + stretch

    second = 3 + g
    steps = jnp.where(g == 0, 4, jnp.where(g < slices - 1, g + 8, g + 7))

    for half in range(halves):
        for each in sends(0, half):
            each.start()

    def step(s, carry):
        slot = lax.rem(s, 2)
        other = 1 - slot
        part = jnp.where(s < 4, s, s - second)
        centre = []
        for r in range(3):
            every = sum(now_at[half, r] for half in range(halves))
            centre.append(jnp.sum(every, keepdims=True) * (1.0 / (blocks * BLOCK)))
        target_features(slot, centre)
        near = order[::-1]
        for half in range(halves):
            source_features(slot, half, me, centre)
        for half in range(halves):
            found = [partner] + [twin(d, -1) for d in near] + [mirror(twin(d, -1)) for d in near]
            for p in found:
                copy(slot, half, p, p, 0).wait_recv()
                source_features(slot, half, p, centre)

        def finish(half):
            now = rates(half, centre)
            current = [now_at[half, r] for r in range(6)]

            def put(values):
                for r in range(6):
                    now_at[half, r] = values[r]
                    for b in range(some):
                        gathered[other, half, me, b, r : r + 1, :] = values[r][b : b + 1, :]

            @pl.when(part == 0)
            def _():
                for r in range(6):
                    base[half, r] = current[r]
                    f0[half, r] = now[r]
                put([current[r] + (0.5 * h) * now[r] for r in range(6)])

            @pl.when(part == 1)
            def _():
                for r in range(6):
                    f1[half, r] = now[r]
                put([current[r] + (0.5 * h) * now[r] for r in range(6)])

            @pl.when(part == 2)
            def _():
                for r in range(6):
                    f2[half, r] = now[r]
                put([
                    base[half, r] + h * (
                        5.0 / 24.0 * f0[half, r] + 1.0 / 3.0 * f1[half, r] - 1.0 / 24.0 * now[r]
                    )
                    for r in range(6)
                ])

            @pl.when(part == 3)
            def _():
                coarse = [base[half, r] + h * f0[half, r] for r in range(6)]
                correction = [
                    current[r]
                    + (0.5 * h) * (now[r] - f1[half, r])
                    + h * (
                        -1.0 / 24.0 * f0[half, r]
                        + 1.0 / 3.0 * f1[half, r]
                        + 5.0 / 24.0 * f2[half, r]
                    )
                    - coarse[r]
                    for r in range(6)
                ]

                @pl.when(s == 3)
                def _():
                    for r in range(6):
                        c0[half, r] = correction[r]

                @pl.when((s > 3) & (g > 1))
                def _():
                    pass_copy(half).wait_recv()
                    put([incoming[half, r] + correction[r] for r in range(6)])

                @pl.when((s == 3) | (g <= 1))
                def _():
                    put([coarse[r] + correction[r] for r in range(6)])

                @pl.when((s > 3) | (g == 0))
                def _():
                    for b in range(some):
                        at = (half * some + b) * BLOCK
                        for r in range(6):
                            out_ref[0, r : r + 1, at : at + BLOCK] = now_at[half, r, b : b + 1, :]

            @pl.when(part < 0)
            def _():
                put([current[r] + h * now[r] + c0[half, r] for r in range(6)])

            @pl.when(part == 4)
            def _():
                for r in range(6):
                    outgoing[half, r] = current[r] + h * now[r]
                pass_copy(half).start()

            @pl.when(s < steps - 1)
            def _():
                for each in sends(other, half):
                    each.start()

        all_targets(finish)
        for half in range(halves):
            for each in sends(slot, half):
                each.wait_send()
        return carry

    lax.fori_loop(0, steps, step, 0)

    @pl.when((g > 0) & (g < slices - 1))
    def _():
        for half in range(halves):
            pass_copy(half).wait_send()


def per_device(spaces, slices, positions, strengths, source_lists, block_slot):
    blocks, width = source_lists.shape
    whole = block_slot.shape[0]
    halves = 2 if blocks % 2 == 0 else 1
    some = blocks // halves
    state = pltpu.VMEM((halves, 6, some, BLOCK), jnp.float32)
    vmem = pl.BlockSpec(memory_space=pltpu.VMEM)
    smem = pl.BlockSpec(memory_space=pltpu.SMEM)
    return pl.pallas_call(
        functools.partial(kernel, spaces, slices, blocks, width, halves),
        out_shape=jax.ShapeDtypeStruct((1, 6, blocks * BLOCK), jnp.float32),
        in_specs=[vmem, vmem, smem, smem],
        out_specs=vmem,
        scratch_shapes=[
            pltpu.VMEM((2, halves, spaces, some, 6, BLOCK), jnp.float32),
            state, state, state, state, state, state, state, state,
            pltpu.VMEM((blocks * TERMS, BLOCK), jnp.float32),
            pltpu.VMEM((whole, DEPTH, BLOCK), jnp.bfloat16),
            pltpu.VMEM((whole, PIECES * TERMS, BLOCK), jnp.bfloat16),
            pltpu.VMEM((blocks, BLOCK, DEPTH), jnp.bfloat16),
            pltpu.SemaphoreType.DMA((2, halves, spaces)),
            pltpu.SemaphoreType.DMA((2, halves, spaces)),
            pltpu.SemaphoreType.DMA((2, halves)),
        ],
        compiler_params=pltpu.CompilerParams(collective_id=0, has_side_effects=True),
    )(positions, strengths, source_lists, block_slot)


def solution(mesh):
    return jax.shard_map(
        functools.partial(per_device, mesh.shape["space"], mesh.shape["tm"]),
        mesh=mesh,
        in_specs=(P(None, "space"), P(None, "space"), P("space", None), P()),
        out_specs=P("tm", None, "space"),
        check_vma=False,
    )
```

```python
import functools

import jax
import jax.numpy as jnp
from jax import lax
from jax.experimental import pallas as pl
from jax.experimental.pallas import tpu as pltpu
from jax.sharding import PartitionSpec as P

BLOCK = 128
SUB = 8
PIECES = 3
TERMS = 32
DEPTH = 32
AHEAD = 6
MESH = pl.DeviceIdType.MESH

time_step = 0.1
core_square = 0.25
inv_four_pi = 0.07957747154594767


def cross(u, v):
    return [
        u[1] * v[2] - u[2] * v[1],
        u[2] * v[0] - u[0] * v[2],
        u[0] * v[1] - u[1] * v[0],
    ]


def dot3(u, v):
    return u[0] * v[0] + u[1] * v[1] + u[2] * v[2]


def rounded(v):
    return v.astype(jnp.bfloat16).astype(jnp.float32)


def split3(v):
    high = rounded(v)
    rest = v - high
    middle = rounded(rest)
    return high, middle, rounded(rest - middle)


def kernel(
    spaces, slices, blocks, width, halves,
    pos_hbm, str_hbm, list_hbm, slot_hbm, out_ref,
    pos_ref, str_ref, list_ref, slot_ref,
    gathered, mine, now_at, base, f0, f1, f2, c0, arriving, outgoing,
    sums, feat, moment, coef, load_sem, send_sem, recv_sem, give_sem, take_sem,
):
    me = lax.axis_index("space")
    g = lax.axis_index("tm")
    h = time_step
    some = blocks // halves

    loads = [
        pltpu.make_async_copy(src, dst, load_sem.at[k])
        for k, (src, dst) in enumerate(
            [(pos_hbm, pos_ref), (str_hbm, str_ref), (list_hbm, list_ref), (slot_hbm, slot_ref)]
        )
    ]
    for each in loads:
        each.start()

    barrier = pltpu.get_barrier_semaphore()

    def greet(d, carry):
        peer = lax.rem(me + d, spaces)
        pl.semaphore_signal(barrier, inc=1, device_id={"space": peer}, device_id_type=MESH)
        return carry

    lax.fori_loop(1, spaces, greet, 0)

    def greet_before(d, carry):
        peer = lax.rem(me + d, spaces)
        pl.semaphore_signal(
            barrier, inc=1, device_id={"space": peer, "tm": g - 1}, device_id_type=MESH
        )
        return carry

    @pl.when((g > 1) & (g < slices - 1))
    def _():
        lax.fori_loop(0, spaces, greet_before, 0)

    @pl.when((g > 1) & (g == slices - 1))
    def _():
        greet_before(0, 0)

    for each in loads:
        each.wait()

    for b in range(blocks):
        cols = slice(b * BLOCK, (b + 1) * BLOCK)
        half, at = divmod(b, some)
        for r in range(3):
            now_at[half, r, at : at + 1, :] = pos_ref[r : r + 1, cols]
            now_at[half, 3 + r, at : at + 1, :] = str_ref[r : r + 1, cols]
            gathered[0, half, me, at, r : r + 1, :] = pos_ref[r : r + 1, cols]
            gathered[0, half, me, at, 3 + r : 4 + r, :] = str_ref[r : r + 1, cols]

    after = jnp.where(g < slices - 2, spaces, jnp.where(g < slices - 1, 1, 0))
    pl.semaphore_wait(barrier, spaces - 1 + jnp.where(g > 0, after, 0))

    chips = spaces // 2
    tall = chips // 2
    core = lax.rem(me, 2)
    column = lax.rem(me // 2, 2)
    row = me // 4
    partner = me + 1 - 2 * core

    def twin(d, sign):
        other_column = lax.rem(column + d % 2, 2)
        other_row = lax.rem(row + tall + sign * (d // 2), tall)
        return 2 * (2 * other_row + other_column) + core

    def copy(slot, half, what, where, sem):
        return pltpu.make_async_remote_copy(
            src_ref=gathered.at[slot, half, what],
            dst_ref=gathered.at[slot, half, what],
            send_sem=send_sem.at[slot, half, sem],
            recv_sem=recv_sem.at[slot, half, what],
            device_id={"space": where},
            device_id_type=MESH,
        )

    order = sorted(range(1, chips), key=lambda d: (-(d % 2) - (d // 2), d))

    def mirror(p):
        return p + 1 - 2 * core

    def sends(slot, half):
        found = []
        for d in order:
            found.append(copy(slot, half, me, twin(d, 1), d))
            found.append(copy(slot, half, me, mirror(twin(d, 1)), chips + d))
        return found + [copy(slot, half, me, partner, 0)]

    def pass_copy(half, what, d):
        return pltpu.make_async_remote_copy(
            src_ref=outgoing.at[half],
            dst_ref=arriving.at[half, what],
            send_sem=give_sem.at[half, d],
            recv_sem=take_sem.at[half, what],
            device_id={"space": lax.rem(me + d, spaces), "tm": lax.rem(g + 1, slices)},
            device_id_type=MESH,
        )

    at_row = lax.broadcasted_iota(jnp.int32, (SUB, BLOCK), 0)

    def stack(values):
        found = values[0]
        for r, v in enumerate(values[1:]):
            found = jnp.where(at_row > r, v, found)
        return found

    def spread(v):
        return jnp.broadcast_to(v, (SUB, BLOCK))

    def source_block(tile, half, p, b, centre):
        rows = [tile[b, r : r + 1, :] for r in range(6)]
        x = [spread(v) - c for v, c in zip(rows[:3], centre)]
        a = [spread(v) for v in rows[3:]]
        square = dot3(x, x)
        six = a + cross(x, a)
        whole = stack([x[0], x[1], x[2], square, jnp.ones_like(square), x[0], x[1], x[2]])
        high, middle, low = split3(whole)
        second = jnp.where((at_row <= 2) | (at_row == 4), high, middle)
        third = jnp.where(at_row == 4, high, jnp.where(at_row <= 2, middle, low))
        at = p * blocks + half * some + b
        feat[at] = jnp.concatenate(
            [high, second, third, jnp.zeros_like(high)], 0
        ).astype(jnp.bfloat16)
        common = stack(six)
        inner = at_row <= 5
        parts = []
        for k in range(3):
            ends = jnp.where(at_row == 6, six[2 * k], six[2 * k + 1])
            parts.append(jnp.where(inner, common * x[k], ends))
        parts.append(common * square)
        pieces = split3(jnp.concatenate(parts, 0))
        moment[at] = jnp.concatenate(pieces, 0).astype(jnp.bfloat16)

    def source_features(tile, half, p, centre):
        for b in range(some):
            source_block(tile, half, p, b, centre)

    def target_features(centre):
        for half in range(halves):
            for b in range(some):
                x = [
                    spread(mine[half, b, r : r + 1, :]) - centre[r]
                    for r in range(3)
                ]
                square = dot3(x, x) + core_square
                minus = [-2.0 * v for v in x]
                high, middle, low = split3(
                    stack(minus + [jnp.ones_like(square), square] + minus)
                )
                first = jnp.where(at_row <= 4, high, middle)
                exact = (at_row == 3) | (at_row >= 5)
                second = jnp.where(exact, high, jnp.where(at_row == 4, middle, low))
                third = jnp.where(exact, high, jnp.where(at_row == 4, low, middle))
                pieces = jnp.concatenate([first, second, third, jnp.zeros_like(first)], 0)
                coef[half * some + b] = pieces.T.astype(jnp.bfloat16)

    group = 2 if width % 2 == 0 else 1

    def pair_product(i, j):
        at = [slot_ref[list_ref[i, j + k]] for k in range(group)]
        right = jnp.concatenate([feat[p] for p in at], 1)
        both = lax.dot_general(
            coef[i], right, (((1,), (0,)), ((), ())), preferred_element_type=jnp.float32
        )
        return at, both

    def pair_sums(at, both):
        inverse = lax.rsqrt(both)
        square = inverse * inverse
        weight = (square * square) * inverse
        high = weight.astype(jnp.bfloat16)
        low = (weight - high.astype(jnp.float32)).astype(jnp.bfloat16)
        moments = jnp.concatenate([moment[p] for p in at], 1)
        return lax.dot_general(
            moments, jnp.concatenate([high, low], 0), (((1,), (1,)), ((), ())),
            preferred_element_type=jnp.float32,
        )

    def all_targets(finish):
        work = [(i, j) for i in range(blocks) for j in range(0, width, group)]
        waiting = []
        total = 0.0
        for k in range(len(work) + AHEAD):
            if k < len(work):
                i, j = work[k]
                waiting.append((i, pair_product(i, j)))
            if k >= AHEAD:
                i, (at, both) = waiting.pop(0)
                total += pair_sums(at, both)
                if k - AHEAD == len(work) - 1 or work[k - AHEAD + 1][0] != i:
                    joined = total[:, :BLOCK] + total[:, BLOCK:]
                    sums[i * TERMS : (i + 1) * TERMS, :] = (
                        joined[2 * TERMS :] + joined[TERMS : 2 * TERMS] + joined[:TERMS]
                    )
                    total = 0.0
                    if (i + 1) % some == 0:
                        finish(i // some)

    def rates(half, centre):
        x = [now_at[half, r] - centre[r] for r in range(3)]
        a = [now_at[half, 3 + r] for r in range(3)]
        pick = lambda r: sums[pl.ds(half * some * TERMS + r, some, stride=TERMS), :]
        plain = [pick(SUB * (c // 2) + 6 + c % 2) for c in range(6)]
        along = [[pick(SUB * k + c) for c in range(6)] for k in range(3)]
        squared = [pick(SUB * 3 + c) for c in range(6)]
        near = dot3(x, x) + core_square
        turn = dot3(a, x)
        three = [
            near * plain[c] - 2.0 * dot3(x, [along[k][c] for k in range(3)]) + squared[c]
            for c in range(6)
        ]
        five = [
            turn * plain[c] - dot3(a, [along[k][c] for k in range(3)]) for c in range(6)
        ]
        cross_v = cross(x, three[:3])
        cross_s = cross(a, three[:3])
        cross_f = cross(x, five[:3])
        velocity = [-inv_four_pi * (cross_v[r] - three[3 + r]) for r in range(3)]
        stretch = [
            -inv_four_pi * (cross_s[r] - 3.0 * (cross_f[r] - five[3 + r])) for r in range(3)
        ]
        return velocity + stretch

    def write_out(half, r, value):
        out_ref[r * blocks + half * some : r * blocks + (half + 1) * some, :] = value

    second = 3 + g
    steps = jnp.where(g == 0, 4, jnp.where(g < slices - 1, g + 8, g + 7))

    for half in range(halves):
        for each in sends(0, half):
            each.start()

    def step(s, carry):
        slot = lax.rem(s, 2)
        other = 1 - slot
        part = jnp.where(s < 4, s, s - second)
        joins = (part == 4) & (g > 1)
        for half in range(halves):
            mine[half] = gathered[slot, half, me]

        @pl.when(joins)
        def _():
            for half in range(halves):
                pass_copy(half, me, 0).wait_recv()
                mine[half] = mine[half] + arriving[half, me]
                for b in range(some):
                    for r in range(6):
                        now_at[half, r, b : b + 1, :] = mine[half, b, r : r + 1, :]
                for r in range(6):
                    write_out(half, r, now_at[half, r])

        centre = []
        for r in range(3):
            every = sum(now_at[half, r] for half in range(halves))
            centre.append(jnp.sum(every, keepdims=True) * (1.0 / (blocks * BLOCK)))
        target_features(centre)
        near = order[::-1]
        for half in range(halves):
            source_features(mine.at[half], half, me, centre)
        for half in range(halves):
            found = [partner] + [twin(d, -1) for d in near] + [mirror(twin(d, -1)) for d in near]
            for p in found:
                copy(slot, half, p, p, 0).wait_recv()

                @pl.when(joins)
                def _():
                    pass_copy(half, p, 0).wait_recv()
                    gathered[slot, half, p] = gathered[slot, half, p] + arriving[half, p]

                source_features(gathered.at[slot, half, p], half, p, centre)

        def finish(half):
            now = rates(half, centre)
            current = [now_at[half, r] for r in range(6)]

            def put(values):
                for r in range(6):
                    now_at[half, r] = values[r]
                    for b in range(some):
                        gathered[other, half, me, b, r : r + 1, :] = values[r][b : b + 1, :]

            @pl.when(part == 0)
            def _():
                for r in range(6):
                    base[half, r] = current[r]
                    f0[half, r] = now[r]
                put([current[r] + (0.5 * h) * now[r] for r in range(6)])

            @pl.when(part == 1)
            def _():
                for r in range(6):
                    f1[half, r] = now[r]
                put([current[r] + (0.5 * h) * now[r] for r in range(6)])

            @pl.when(part == 2)
            def _():
                for r in range(6):
                    f2[half, r] = now[r]
                put([
                    base[half, r] + h * (
                        5.0 / 24.0 * f0[half, r] + 1.0 / 3.0 * f1[half, r] - 1.0 / 24.0 * now[r]
                    )
                    for r in range(6)
                ])

            @pl.when(part == 3)
            def _():
                coarse = [base[half, r] + h * f0[half, r] for r in range(6)]
                correction = [
                    current[r]
                    + (0.5 * h) * (now[r] - f1[half, r])
                    + h * (
                        -1.0 / 24.0 * f0[half, r]
                        + 1.0 / 3.0 * f1[half, r]
                        + 5.0 / 24.0 * f2[half, r]
                    )
                    - coarse[r]
                    for r in range(6)
                ]

                @pl.when(s == 3)
                def _():
                    for r in range(6):
                        c0[half, r] = correction[r]

                @pl.when((s > 3) & (g > 1) & (g < slices - 1))
                def _():
                    put(correction)

                @pl.when((s > 3) & (g > 1) & (g == slices - 1))
                def _():
                    pass_copy(half, me, 0).wait_recv()
                    for b in range(some):
                        for r in range(6):
                            outgoing[half, b, r : r + 1, :] = correction[r][b : b + 1, :]
                            at = r * blocks + half * some + b
                            out_ref[at : at + 1, :] = (
                                arriving[half, me, b, r : r + 1, :]
                                + outgoing[half, b, r : r + 1, :]
                            )

                @pl.when((s == 3) | (g <= 1))
                def _():
                    put([coarse[r] + correction[r] for r in range(6)])

                @pl.when(((s > 3) & (g == 1)) | (g == 0))
                def _():
                    for r in range(6):
                        write_out(half, r, coarse[r] + correction[r])

            @pl.when(part < 0)
            def _():
                put([current[r] + h * now[r] + c0[half, r] for r in range(6)])

            @pl.when(part == 4)
            def _():
                for r in range(6):
                    value = current[r] + h * now[r]
                    for b in range(some):
                        outgoing[half, b, r : r + 1, :] = value[b : b + 1, :]
                pass_copy(half, me, 0).start()

                @pl.when(g < slices - 2)
                def _():
                    for d in range(1, spaces):
                        pass_copy(half, me, d).start()

            @pl.when(s < steps - 1)
            def _():
                for each in sends(other, half):
                    each.start()

        all_targets(finish)
        for half in range(halves):
            for each in sends(slot, half):
                each.wait_send()
        return carry

    lax.fori_loop(0, steps, step, 0)

    @pl.when((g > 0) & (g < slices - 1))
    def _():
        for half in range(halves):
            pass_copy(half, me, 0).wait_send()

    @pl.when((g > 0) & (g < slices - 2))
    def _():
        for half in range(halves):
            for d in range(1, spaces):
                pass_copy(half, me, d).wait_send()


def per_device(spaces, slices, positions, strengths, source_lists, block_slot):
    blocks, width = source_lists.shape
    whole = block_slot.shape[0]
    halves = 2 if blocks % 2 == 0 else 1
    some = blocks // halves
    state = pltpu.VMEM((halves, 6, some, BLOCK), jnp.float32)
    tiles = (some, 6, BLOCK)
    anywhere = pl.BlockSpec(memory_space=pl.ANY)
    out = pl.pallas_call(
        functools.partial(kernel, spaces, slices, blocks, width, halves),
        out_shape=jax.ShapeDtypeStruct((6 * blocks, BLOCK), jnp.float32),
        in_specs=[anywhere] * 4,
        out_specs=pl.BlockSpec(memory_space=pltpu.VMEM),
        scratch_shapes=[
            pltpu.VMEM(positions.shape, jnp.float32),
            pltpu.VMEM(strengths.shape, jnp.float32),
            pltpu.SMEM(source_lists.shape, jnp.int32),
            pltpu.SMEM(block_slot.shape, jnp.int32),
            pltpu.VMEM((2, halves, spaces) + tiles, jnp.float32),
            pltpu.VMEM((halves,) + tiles, jnp.float32),
            state, state, state, state, state, state,
            pltpu.VMEM((halves, spaces) + tiles, jnp.float32),
            pltpu.VMEM((halves,) + tiles, jnp.float32),
            pltpu.VMEM((blocks * TERMS, BLOCK), jnp.float32),
            pltpu.VMEM((whole, DEPTH, BLOCK), jnp.bfloat16),
            pltpu.VMEM((whole, PIECES * TERMS, BLOCK), jnp.bfloat16),
            pltpu.VMEM((blocks, BLOCK, DEPTH), jnp.bfloat16),
            pltpu.SemaphoreType.DMA((4,)),
            pltpu.SemaphoreType.DMA((2, halves, spaces)),
            pltpu.SemaphoreType.DMA((2, halves, spaces)),
            pltpu.SemaphoreType.DMA((halves, spaces)),
            pltpu.SemaphoreType.DMA((halves, spaces)),
        ],
        compiler_params=pltpu.CompilerParams(collective_id=0, has_side_effects=True),
    )(positions, strengths, source_lists, block_slot)
    return out.reshape(1, 6, blocks * BLOCK)


def solution(mesh):
    return jax.shard_map(
        functools.partial(per_device, mesh.shape["space"], mesh.shape["tm"]),
        mesh=mesh,
        in_specs=(P(None, "space"), P(None, "space"), P("space", None), P()),
        out_specs=P("tm", None, "space"),
        check_vma=False,
    )
```

```python
import functools

import jax
import jax.numpy as jnp
from jax import lax
from jax.experimental import pallas as pl
from jax.experimental.pallas import tpu as pltpu
from jax.sharding import PartitionSpec as P

BLOCK = 128
SUB = 8
PIECES = 3
TERMS = 32
DEPTH = 32
AHEAD = 6
MESH = pl.DeviceIdType.MESH

time_step = 0.1
core_square = 0.25
inv_four_pi = 0.07957747154594767


def cross(u, v):
    return [
        u[1] * v[2] - u[2] * v[1],
        u[2] * v[0] - u[0] * v[2],
        u[0] * v[1] - u[1] * v[0],
    ]


def dot3(u, v):
    return u[0] * v[0] + u[1] * v[1] + u[2] * v[2]


def rounded(v):
    return v.astype(jnp.bfloat16).astype(jnp.float32)


def split3(v):
    high = rounded(v)
    rest = v - high
    middle = rounded(rest)
    return high, middle, rounded(rest - middle)


def kernel(
    spaces, slices, blocks, width, pieces, paired,
    pos_hbm, str_hbm, list_hbm, slot_hbm, out_ref,
    pos_ref, str_ref, list_ref, slot_ref,
    gathered, crossing, mine, rate, final, base, f0, f1, f2, c0, arriving, outgoing,
    sums, feat, moment, coef, load_sem, send_sem, cross_sem, recv_sem, give_sem, take_sem,
):
    me = lax.axis_index("space")
    g = lax.axis_index("tm")
    h = time_step
    some = blocks // pieces
    pair = pieces // 2
    q = lax.rem(g, 2) if paired else 0
    other_plane = g + 1 - 2 * q
    shared_last = 3 + 2 * (g // 2) if paired else -1

    loads = [
        pltpu.make_async_copy(src, dst, load_sem.at[k])
        for k, (src, dst) in enumerate(
            [(pos_hbm, pos_ref), (str_hbm, str_ref), (list_hbm, list_ref), (slot_hbm, slot_ref)]
        )
    ]
    for each in loads:
        each.start()

    barrier = pltpu.get_barrier_semaphore()

    def greet(d, carry):
        peer = lax.rem(me + d, spaces)
        pl.semaphore_signal(barrier, inc=1, device_id={"space": peer}, device_id_type=MESH)
        return carry

    lax.fori_loop(1, spaces, greet, 0)

    def greet_before(d, carry):
        peer = lax.rem(me + d, spaces)
        pl.semaphore_signal(
            barrier, inc=1, device_id={"space": peer, "tm": g - 1}, device_id_type=MESH
        )
        return carry

    def greet_across(d, carry):
        peer = lax.rem(me + d, spaces)
        pl.semaphore_signal(
            barrier, inc=1, device_id={"space": peer, "tm": other_plane}, device_id_type=MESH
        )
        return carry

    if paired:
        lax.fori_loop(0, spaces, greet_across, 0)

    @pl.when((g > 1) & (g < slices - 1))
    def _():
        lax.fori_loop(0, spaces, greet_before, 0)

    @pl.when((g > 1) & (g == slices - 1))
    def _():
        greet_before(0, 0)

    for each in loads:
        each.wait()

    for b in range(blocks):
        cols = slice(b * BLOCK, (b + 1) * BLOCK)
        piece, at = divmod(b, some)
        for r in range(3):
            gathered[0, piece, me, at, r : r + 1, :] = pos_ref[r : r + 1, cols]
            gathered[0, piece, me, at, 3 + r : 4 + r, :] = str_ref[r : r + 1, cols]

    after = jnp.where(g < slices - 2, spaces, jnp.where(g < slices - 1, 1, 0))
    pl.semaphore_wait(barrier, spaces - 1 + (spaces if paired else 0) + jnp.where(g > 0, after, 0))

    chips = spaces // 2
    tall = chips // 2
    core = lax.rem(me, 2)
    column = lax.rem(me // 2, 2)
    row = me // 4
    partner = me + 1 - 2 * core

    def twin(d, sign):
        other_column = lax.rem(column + d % 2, 2)
        other_row = lax.rem(row + tall + sign * (d // 2), tall)
        return 2 * (2 * other_row + other_column) + core

    def copy(slot, t, what, where, sem):
        return pltpu.make_async_remote_copy(
            src_ref=gathered.at[slot, t, what],
            dst_ref=gathered.at[slot, t, what],
            send_sem=send_sem.at[slot, t, sem],
            recv_sem=recv_sem.at[slot, t, what],
            device_id={"space": where},
            device_id_type=MESH,
        )

    def cross_copy(slot, u, d):
        t = 2 * u + q
        return pltpu.make_async_remote_copy(
            src_ref=crossing.at[slot, u],
            dst_ref=gathered.at[slot, t, me],
            send_sem=cross_sem.at[slot, u, d],
            recv_sem=recv_sem.at[slot, t, me],
            device_id={"space": lax.rem(me + d, spaces), "tm": other_plane},
            device_id_type=MESH,
        )

    order = sorted(range(1, chips), key=lambda d: (-(d % 2) - (d // 2), d))

    def mirror(p):
        return p + 1 - 2 * core

    def sends(slot, t):
        found = []
        for d in order:
            found.append(copy(slot, t, me, twin(d, 1), d))
            found.append(copy(slot, t, me, mirror(twin(d, 1)), chips + d))
        return found + [copy(slot, t, me, partner, 0)]

    cross_order = list(range(spaces - 1, -1, -1))

    def pass_copy(t, what, d):
        return pltpu.make_async_remote_copy(
            src_ref=outgoing.at[t],
            dst_ref=arriving.at[t, what],
            send_sem=give_sem.at[t, d],
            recv_sem=take_sem.at[t, what],
            device_id={"space": lax.rem(me + d, spaces), "tm": lax.rem(g + 1, slices)},
            device_id_type=MESH,
        )

    at_row = lax.broadcasted_iota(jnp.int32, (SUB, BLOCK), 0)

    def stack(values):
        found = values[0]
        for r, v in enumerate(values[1:]):
            found = jnp.where(at_row > r, v, found)
        return found

    def spread(v):
        return jnp.broadcast_to(v, (SUB, BLOCK))

    def source_block(tile, t, p, b, centre):
        rows = [tile[b, r : r + 1, :] for r in range(6)]
        x = [spread(v) - c for v, c in zip(rows[:3], centre)]
        a = [spread(v) for v in rows[3:]]
        square = dot3(x, x)
        six = a + cross(x, a)
        whole = stack([x[0], x[1], x[2], square, jnp.ones_like(square), x[0], x[1], x[2]])
        high, middle, low = split3(whole)
        second = jnp.where((at_row <= 2) | (at_row == 4), high, middle)
        third = jnp.where(at_row == 4, high, jnp.where(at_row <= 2, middle, low))
        at = p * blocks + t * some + b
        feat[at] = jnp.concatenate(
            [high, second, third, jnp.zeros_like(high)], 0
        ).astype(jnp.bfloat16)
        common = stack(six)
        inner = at_row <= 5
        parts = []
        for k in range(3):
            ends = jnp.where(at_row == 6, six[2 * k], six[2 * k + 1])
            parts.append(jnp.where(inner, common * x[k], ends))
        parts.append(common * square)
        pieces = split3(jnp.concatenate(parts, 0))
        moment[at] = jnp.concatenate(pieces, 0).astype(jnp.bfloat16)

    def source_features(tile, t, p, centre):
        for b in range(some):
            source_block(tile, t, p, b, centre)

    def target_features(t, centre):
        for b in range(some):
            x = [spread(mine[t, b, r : r + 1, :]) - centre[r] for r in range(3)]
            square = dot3(x, x) + core_square
            minus = [-2.0 * v for v in x]
            high, middle, low = split3(
                stack(minus + [jnp.ones_like(square), square] + minus)
            )
            first = jnp.where(at_row <= 4, high, middle)
            exact = (at_row == 3) | (at_row >= 5)
            second = jnp.where(exact, high, jnp.where(at_row == 4, middle, low))
            third = jnp.where(exact, high, jnp.where(at_row == 4, low, middle))
            rows = jnp.concatenate([first, second, third, jnp.zeros_like(first)], 0)
            coef[t * some + b] = rows.T.astype(jnp.bfloat16)

    group = 2 if width % 2 == 0 else 1

    def pair_product(i, j):
        at = [slot_ref[list_ref[i, j + k]] for k in range(group)]
        right = jnp.concatenate([feat[p] for p in at], 1)
        both = lax.dot_general(
            coef[i], right, (((1,), (0,)), ((), ())), preferred_element_type=jnp.float32
        )
        return at, both

    def pair_sums(at, both):
        inverse = lax.rsqrt(both)
        square = inverse * inverse
        weight = (square * square) * inverse
        high = weight.astype(jnp.bfloat16)
        low = (weight - high.astype(jnp.float32)).astype(jnp.bfloat16)
        moments = jnp.concatenate([moment[p] for p in at], 1)
        return lax.dot_general(
            moments, jnp.concatenate([high, low], 0), (((1,), (1,)), ((), ())),
            preferred_element_type=jnp.float32,
        )

    def some_targets(chosen, finish):
        work = [(n, j) for n in range(len(chosen) * some) for j in range(0, width, group)]
        waiting = []
        total = 0.0
        for k in range(len(work) + AHEAD):
            if k < len(work):
                n, j = work[k]
                waiting.append((n, pair_product(chosen[n // some] * some + n % some, j)))
            if k >= AHEAD:
                n, (at, both) = waiting.pop(0)
                total += pair_sums(at, both)
                if k - AHEAD == len(work) - 1 or work[k - AHEAD + 1][0] != n:
                    joined = total[:, :BLOCK] + total[:, BLOCK:]
                    sums[n * TERMS : (n + 1) * TERMS, :] = (
                        joined[2 * TERMS :] + joined[TERMS : 2 * TERMS] + joined[:TERMS]
                    )
                    total = 0.0
                    if (n + 1) % some == 0:
                        finish(n // some, chosen[n // some])

    def rates(u, t, centre):
        row = lambda r: jnp.concatenate([mine[t, b, r : r + 1, :] for b in range(some)], 0)
        x = [row(r) - centre[r] for r in range(3)]
        a = [row(3 + r) for r in range(3)]
        pick = lambda r: sums[pl.ds(u * some * TERMS + r, some, stride=TERMS), :]
        plain = [pick(SUB * (c // 2) + 6 + c % 2) for c in range(6)]
        along = [[pick(SUB * k + c) for c in range(6)] for k in range(3)]
        squared = [pick(SUB * 3 + c) for c in range(6)]
        near = dot3(x, x) + core_square
        turn = dot3(a, x)
        three = [
            near * plain[c] - 2.0 * dot3(x, [along[k][c] for k in range(3)]) + squared[c]
            for c in range(6)
        ]
        five = [
            turn * plain[c] - dot3(a, [along[k][c] for k in range(3)]) for c in range(6)
        ]
        cross_v = cross(x, three[:3])
        cross_s = cross(a, three[:3])
        cross_f = cross(x, five[:3])
        velocity = [-inv_four_pi * (cross_v[r] - three[3 + r]) for r in range(3)]
        stretch = [
            -inv_four_pi * (cross_s[r] - 3.0 * (cross_f[r] - five[3 + r])) for r in range(3)
        ]
        for r, v in enumerate(velocity + stretch):
            for b in range(some):
                rate[u, b, r : r + 1, :] = v[b : b + 1, :]

    second = 3 + g
    steps = jnp.where(g == 0, 4, jnp.where(g < slices - 1, g + 8, g + 7))

    for t in range(pieces):
        for each in sends(0, t):
            each.start()

    def step(s, carry):
        slot = lax.rem(s, 2)
        other = 1 - slot
        part = jnp.where(s < 4, s, s - second)
        joins = (part == 4) & (g > 1)
        shared = s <= shared_last
        crossed = (s > 0) & (s <= shared_last + 1)
        own = [2 * u + q for u in range(pair)] if paired else list(range(pieces))
        for t in own:
            mine[t] = gathered[slot, t, me]

        if not paired:
            rest = []
        else:
            rest = [2 * u + 1 - q for u in range(pair)]

            @pl.when(jnp.logical_not(crossed))
            def _():
                for t in rest:
                    mine[t] = gathered[slot, t, me]

        @pl.when(joins)
        def _():
            for t in range(pieces):
                pass_copy(t, me, 0).wait_recv()
                mine[t] = mine[t] + arriving[t, me]
                final[t] = mine[t]

        centre = []
        for r in range(3):
            every = sum(mine[t, b, r : r + 1, :] for t in own for b in range(some))
            centre.append(
                jnp.sum(every, keepdims=True) * (1.0 / (len(own) * some * BLOCK))
            )
        for t in own:
            target_features(t, centre)
            source_features(mine.at[t], t, me, centre)
        near = order[::-1]
        found = [partner]
        for d in near:
            found += [twin(d, -1), mirror(twin(d, -1))]
        for u in range(max(pair, 1)):
            if paired:
                t = rest[u]

                @pl.when(crossed)
                def _():
                    copy(slot, t, me, partner, 0).wait_recv()

                    @pl.when((part == 1) & (s > 3))
                    def _():
                        base[t] = mine[t]
                        f0[t] = (gathered[slot, t, me] - mine[t]) * (2.0 / h)

                    mine[t] = gathered[slot, t, me]

                target_features(t, centre)
                source_features(mine.at[t], t, me, centre)
            for p in found:
                for v in range(2 if pair else 1):
                    t = 2 * u + v
                    copy(slot, t, p, p, 0).wait_recv()

                    @pl.when(joins)
                    def _():
                        pass_copy(t, p, 0).wait_recv()
                        gathered[slot, t, p] = gathered[slot, t, p] + arriving[t, p]

                    source_features(gathered.at[slot, t, p], t, p, centre)

        def finish(u, t):
            rates(u, t, centre)
            now = rate[u]
            current = mine[t]

            def put(value, across=None):
                gathered[other, t, me] = value
                if paired:

                    @pl.when(shared)
                    def _():
                        crossing[other, u] = value if across is None else across

            @pl.when(part == 0)
            def _():
                base[t] = current
                f0[t] = now
                half_step = current + (0.5 * h) * now

                @pl.when(s == 0)
                def _():
                    put(half_step)

                @pl.when(s > 0)
                def _():
                    put(half_step, current + h * now + c0[t])

            @pl.when(part == 1)
            def _():
                f1[t] = now
                put(current + (0.5 * h) * now)

            @pl.when(part == 2)
            def _():
                f2[t] = now
                put(
                    base[t]
                    + h * (5.0 / 24.0 * f0[t] + 1.0 / 3.0 * f1[t] - 1.0 / 24.0 * now)
                )

            @pl.when(part == 3)
            def _():
                coarse = base[t] + h * f0[t]
                correction = (
                    current
                    + (0.5 * h) * (now - f1[t])
                    + h * (-1.0 / 24.0 * f0[t] + 1.0 / 3.0 * f1[t] + 5.0 / 24.0 * f2[t])
                    - coarse
                )

                @pl.when(s == 3)
                def _():
                    c0[t] = correction

                @pl.when((s > 3) & (g > 1) & (g < slices - 1))
                def _():
                    put(correction)

                @pl.when((s > 3) & (g > 1) & (g == slices - 1))
                def _():
                    pass_copy(t, me, 0).wait_recv()
                    final[t] = arriving[t, me] + correction

                @pl.when((s == 3) | (g <= 1))
                def _():
                    put(coarse + correction)
                    final[t] = coarse + correction

            @pl.when((part < 0) & (s < shared_last))
            def _():
                put(current + h * now + c0[t])

            @pl.when((part < 0) & (s >= shared_last))
            def _():
                put(current + h * now + c0[t], current + (0.5 * h) * now)

            @pl.when(part == 4)
            def _():
                outgoing[t] = current + h * now
                pass_copy(t, me, 0).start()

                @pl.when(g < slices - 2)
                def _():
                    for d in range(1, spaces):
                        pass_copy(t, me, d).start()

            if paired:

                @pl.when(shared)
                def _():
                    for d in cross_order:
                        cross_copy(other, u, d).start()

            @pl.when(s < steps - 1)
            def _():
                for each in sends(other, t):
                    each.start()

        def body(c, carry):
            if paired:
                some_targets([jnp.where(shared, 2 * u + q, 2 * c + u) for u in range(2)], finish)
            else:
                some_targets([c], finish)
            return carry

        if paired:

            @pl.when(s == 0)
            def _():
                for t in range(pieces):
                    for each in sends(slot, t):
                        each.wait_send()

            lax.fori_loop(0, jnp.where(shared, 1, pair), body, 0)
        else:
            for t in range(pieces):
                body(t, 0)

        if paired:

            @pl.when(crossed)
            def _():
                for u in range(pair):
                    for each in sends(slot, 2 * u + q):
                        each.wait_send()
                    for d in cross_order:
                        cross_copy(slot, u, d).wait_send()

            @pl.when(jnp.logical_not(crossed) & (s > 0))
            def _():
                for t in range(pieces):
                    for each in sends(slot, t):
                        each.wait_send()

        else:
            for t in range(pieces):
                for each in sends(slot, t):
                    each.wait_send()
        return carry

    lax.fori_loop(0, steps, step, 0)

    if paired:

        @pl.when(g == 0)
        def _():
            for u in range(pair):
                t = 2 * u + 1 - q
                for p in [me, partner] + [twin(d, -1) for d in order] + [
                    mirror(twin(d, -1)) for d in order
                ]:
                    copy(0, t, p, partner, 0).wait_recv()
                final[t] = gathered[0, t, me]
                for d in cross_order:
                    cross_copy(0, u, d).wait_send()

    for t in range(pieces):
        for b in range(some):
            for r in range(6):
                at = r * blocks + t * some + b
                out_ref[at : at + 1, :] = final[t, b, r : r + 1, :]

    @pl.when((g > 0) & (g < slices - 1))
    def _():
        for t in range(pieces):
            pass_copy(t, me, 0).wait_send()

    @pl.when((g > 0) & (g < slices - 2))
    def _():
        for t in range(pieces):
            for d in range(1, spaces):
                pass_copy(t, me, d).wait_send()


def per_device(spaces, slices, positions, strengths, source_lists, block_slot):
    blocks, width = source_lists.shape
    whole = block_slot.shape[0]
    paired = blocks % 4 == 0 and slices % 2 == 0
    pieces = 4 if paired else 1
    pair = pieces // 2 if paired else 1
    tiles = (blocks // pieces, 6, BLOCK)
    state = pltpu.VMEM((pieces,) + tiles, jnp.float32)
    anywhere = pl.BlockSpec(memory_space=pl.ANY)
    out = pl.pallas_call(
        functools.partial(kernel, spaces, slices, blocks, width, pieces, paired),
        out_shape=jax.ShapeDtypeStruct((6 * blocks, BLOCK), jnp.float32),
        in_specs=[anywhere] * 4,
        out_specs=pl.BlockSpec(memory_space=pltpu.VMEM),
        scratch_shapes=[
            pltpu.VMEM(positions.shape, jnp.float32),
            pltpu.VMEM(strengths.shape, jnp.float32),
            pltpu.SMEM(source_lists.shape, jnp.int32),
            pltpu.SMEM(block_slot.shape, jnp.int32),
            pltpu.VMEM((2, pieces, spaces) + tiles, jnp.float32),
            pltpu.VMEM((2, pair) + tiles, jnp.float32),
            state,
            pltpu.VMEM((2,) + tiles, jnp.float32),
            state, state, state, state, state, state,
            pltpu.VMEM((pieces, spaces) + tiles, jnp.float32),
            state,
            pltpu.VMEM((blocks * TERMS, BLOCK), jnp.float32),
            pltpu.VMEM((whole, DEPTH, BLOCK), jnp.bfloat16),
            pltpu.VMEM((whole, PIECES * TERMS, BLOCK), jnp.bfloat16),
            pltpu.VMEM((blocks, BLOCK, DEPTH), jnp.bfloat16),
            pltpu.SemaphoreType.DMA((4,)),
            pltpu.SemaphoreType.DMA((2, pieces, spaces)),
            pltpu.SemaphoreType.DMA((2, pair, spaces)),
            pltpu.SemaphoreType.DMA((2, pieces, spaces)),
            pltpu.SemaphoreType.DMA((pieces, spaces)),
            pltpu.SemaphoreType.DMA((pieces, spaces)),
        ],
        compiler_params=pltpu.CompilerParams(collective_id=0, has_side_effects=True),
    )(positions, strengths, source_lists, block_slot)
    return out.reshape(1, 6, blocks * BLOCK)


def solution(mesh):
    return jax.shard_map(
        functools.partial(per_device, mesh.shape["space"], mesh.shape["tm"]),
        mesh=mesh,
        in_specs=(P(None, "space"), P(None, "space"), P("space", None), P()),
        out_specs=P("tm", None, "space"),
        check_vma=False,
    )
```

```python
import functools

import jax
import jax.numpy as jnp
from jax import lax
from jax.experimental import pallas as pl
from jax.experimental.pallas import tpu as pltpu
from jax.sharding import PartitionSpec as P

BLOCK = 128
SUB = 8
PIECES = 3
TERMS = 32
DEPTH = 32
AHEAD = 6
MESH = pl.DeviceIdType.MESH

time_step = 0.1
core_square = 0.25
inv_four_pi = 0.07957747154594767


def cross(u, v):
    return [
        u[1] * v[2] - u[2] * v[1],
        u[2] * v[0] - u[0] * v[2],
        u[0] * v[1] - u[1] * v[0],
    ]


def dot3(u, v):
    return u[0] * v[0] + u[1] * v[1] + u[2] * v[2]


def rounded(v):
    return v.astype(jnp.bfloat16).astype(jnp.float32)


def split3(v):
    high = rounded(v)
    rest = v - high
    middle = rounded(rest)
    return high, middle, rounded(rest - middle)


def kernel(
    spaces, slices, blocks, width, pieces,
    pos_hbm, str_hbm, list_hbm, slot_hbm, out_ref,
    pos_ref, str_ref, list_ref, slot_ref,
    gathered, mine, rate, final, base, f0, f1, f2, c0, arriving, outgoing,
    sums, feat, moment, coef, load_sem, send_sem, recv_sem, give_sem, take_sem,
):
    me = lax.axis_index("space")
    g = lax.axis_index("tm")
    h = time_step
    some = blocks // pieces
    last = pieces - 1

    loads = [
        pltpu.make_async_copy(src, dst, load_sem.at[k])
        for k, (src, dst) in enumerate(
            [(pos_hbm, pos_ref), (str_hbm, str_ref), (list_hbm, list_ref), (slot_hbm, slot_ref)]
        )
    ]
    for each in loads:
        each.start()

    barrier = pltpu.get_barrier_semaphore()

    def greet(d, carry):
        peer = lax.rem(me + d, spaces)
        pl.semaphore_signal(barrier, inc=1, device_id={"space": peer}, device_id_type=MESH)
        return carry

    lax.fori_loop(1, spaces, greet, 0)

    def greet_before(d, carry):
        peer = lax.rem(me + d, spaces)
        pl.semaphore_signal(
            barrier, inc=1, device_id={"space": peer, "tm": g - 1}, device_id_type=MESH
        )
        return carry

    @pl.when((g > 1) & (g < slices - 1))
    def _():
        lax.fori_loop(0, spaces, greet_before, 0)

    @pl.when((g > 1) & (g == slices - 1))
    def _():
        greet_before(0, 0)

    for each in loads:
        each.wait()

    for b in range(blocks):
        cols = slice(b * BLOCK, (b + 1) * BLOCK)
        piece, at = divmod(b, some)
        for r in range(3):
            gathered[0, piece, me, at, r : r + 1, :] = pos_ref[r : r + 1, cols]
            gathered[0, piece, me, at, 3 + r : 4 + r, :] = str_ref[r : r + 1, cols]

    after = jnp.where(g < slices - 2, spaces, jnp.where(g < slices - 1, 1, 0))
    pl.semaphore_wait(barrier, spaces - 1 + jnp.where(g > 0, after, 0))

    chips = spaces // 2
    tall = chips // 2
    core = lax.rem(me, 2)
    column = lax.rem(me // 2, 2)
    row = me // 4
    partner = me + 1 - 2 * core

    def twin(d, sign):
        other_column = lax.rem(column + d % 2, 2)
        other_row = lax.rem(row + tall + sign * (d // 2), tall)
        return 2 * (2 * other_row + other_column) + core

    def copy(slot, t, what, where, sem):
        return pltpu.make_async_remote_copy(
            src_ref=gathered.at[slot, t, what],
            dst_ref=gathered.at[slot, t, what],
            send_sem=send_sem.at[slot, t, sem],
            recv_sem=recv_sem.at[slot, t, what],
            device_id={"space": where},
            device_id_type=MESH,
        )

    order = sorted(range(1, chips), key=lambda d: (-(d % 2) - (d // 2), d))

    def mirror(p):
        return p + 1 - 2 * core

    def sends(slot, t):
        found = []
        for d in order:
            found.append(copy(slot, t, me, twin(d, 1), d))
            found.append(copy(slot, t, me, mirror(twin(d, 1)), chips + d))
        return found + [copy(slot, t, me, partner, 0)]

    def pass_copy(t, what, d):
        return pltpu.make_async_remote_copy(
            src_ref=outgoing.at[t],
            dst_ref=arriving.at[t, what],
            send_sem=give_sem.at[t, d],
            recv_sem=take_sem.at[t, what],
            device_id={"space": lax.rem(me + d, spaces), "tm": lax.rem(g + 1, slices)},
            device_id_type=MESH,
        )

    at_row = lax.broadcasted_iota(jnp.int32, (SUB, BLOCK), 0)

    def stack(values):
        found = values[0]
        for r, v in enumerate(values[1:]):
            found = jnp.where(at_row > r, v, found)
        return found

    def spread(v):
        return jnp.broadcast_to(v, (SUB, BLOCK))

    def source_block(tile, t, p, b, centre):
        rows = [tile[b, r : r + 1, :] for r in range(6)]
        x = [spread(v) - c for v, c in zip(rows[:3], centre)]
        a = [spread(v) for v in rows[3:]]
        square = dot3(x, x)
        six = a + cross(x, a)
        whole = stack([x[0], x[1], x[2], square, jnp.ones_like(square), x[0], x[1], x[2]])
        high, middle, low = split3(whole)
        second = jnp.where((at_row <= 2) | (at_row == 4), high, middle)
        third = jnp.where(at_row == 4, high, jnp.where(at_row <= 2, middle, low))
        at = p * blocks + t * some + b
        feat[at] = jnp.concatenate(
            [high, second, third, jnp.zeros_like(high)], 0
        ).astype(jnp.bfloat16)
        common = stack(six)
        inner = at_row <= 5
        parts = []
        for k in range(3):
            ends = jnp.where(at_row == 6, six[2 * k], six[2 * k + 1])
            parts.append(jnp.where(inner, common * x[k], ends))
        parts.append(common * square)
        pieces = split3(jnp.concatenate(parts, 0))
        moment[at] = jnp.concatenate(pieces, 0).astype(jnp.bfloat16)

    def source_features(tile, t, p, centre):
        for b in range(some):
            source_block(tile, t, p, b, centre)

    def target_features(t, centre):
        for b in range(some):
            x = [spread(mine[t, b, r : r + 1, :]) - centre[r] for r in range(3)]
            square = dot3(x, x) + core_square
            minus = [-2.0 * v for v in x]
            high, middle, low = split3(
                stack(minus + [jnp.ones_like(square), square] + minus)
            )
            first = jnp.where(at_row <= 4, high, middle)
            exact = (at_row == 3) | (at_row >= 5)
            second = jnp.where(exact, high, jnp.where(at_row == 4, middle, low))
            third = jnp.where(exact, high, jnp.where(at_row == 4, low, middle))
            rows = jnp.concatenate([first, second, third, jnp.zeros_like(first)], 0)
            coef[t * some + b] = rows.T.astype(jnp.bfloat16)

    group = 2 if width % 2 == 0 else 1

    def pair_product(i, j):
        at = [slot_ref[list_ref[i, j + k]] for k in range(group)]
        right = jnp.concatenate([feat[p] for p in at], 1)
        both = lax.dot_general(
            coef[i], right, (((1,), (0,)), ((), ())), preferred_element_type=jnp.float32
        )
        return at, both

    def pair_sums(at, both):
        inverse = lax.rsqrt(both)
        square = inverse * inverse
        weight = (square * square) * inverse
        high = weight.astype(jnp.bfloat16)
        low = (weight - high.astype(jnp.float32)).astype(jnp.bfloat16)
        moments = jnp.concatenate([moment[p] for p in at], 1)
        rows = (((1,), (1,)), ((), ()))
        return lax.dot_general(
            moments, high, rows, preferred_element_type=jnp.float32
        ) + lax.dot_general(moments, low, rows, preferred_element_type=jnp.float32)

    def some_targets(chosen, finish):
        work = [(n, j) for n in range(len(chosen) * some) for j in range(0, width, group)]
        waiting = []
        total = 0.0
        for k in range(len(work) + AHEAD):
            if k < len(work):
                n, j = work[k]
                waiting.append((n, pair_product(chosen[n // some] * some + n % some, j)))
            if k >= AHEAD:
                n, (at, both) = waiting.pop(0)
                total += pair_sums(at, both)
                if k - AHEAD == len(work) - 1 or work[k - AHEAD + 1][0] != n:
                    sums[n * TERMS : (n + 1) * TERMS, :] = (
                        total[2 * TERMS :] + total[TERMS : 2 * TERMS] + total[:TERMS]
                    )
                    total = 0.0
                    if (n + 1) % some == 0:
                        finish(n // some, chosen[n // some])

    def rates(u, t, centre):
        row = lambda r: jnp.concatenate([mine[t, b, r : r + 1, :] for b in range(some)], 0)
        x = [row(r) - centre[r] for r in range(3)]
        a = [row(3 + r) for r in range(3)]
        pick = lambda r: sums[pl.ds(u * some * TERMS + r, some, stride=TERMS), :]
        plain = [pick(SUB * (c // 2) + 6 + c % 2) for c in range(6)]
        along = [[pick(SUB * k + c) for c in range(6)] for k in range(3)]
        squared = [pick(SUB * 3 + c) for c in range(6)]
        near = dot3(x, x) + core_square
        turn = dot3(a, x)
        three = [
            near * plain[c] - 2.0 * dot3(x, [along[k][c] for k in range(3)]) + squared[c]
            for c in range(6)
        ]
        five = [
            turn * plain[c] - dot3(a, [along[k][c] for k in range(3)]) for c in range(6)
        ]
        cross_v = cross(x, three[:3])
        cross_s = cross(a, three[:3])
        cross_f = cross(x, five[:3])
        velocity = [-inv_four_pi * (cross_v[r] - three[3 + r]) for r in range(3)]
        stretch = [
            -inv_four_pi * (cross_s[r] - 3.0 * (cross_f[r] - five[3 + r])) for r in range(3)
        ]
        for r, v in enumerate(velocity + stretch):
            for b in range(some):
                rate[u, b, r : r + 1, :] = v[b : b + 1, :]

    second = 3 + g
    steps = jnp.where(g == 0, 4, jnp.where(g < slices - 1, g + 8, g + 7))

    for t in range(pieces):
        for each in sends(0, t):
            each.start()

    def step(s, carry):
        slot = lax.rem(s, 2)
        other = 1 - slot
        part = jnp.where(s < 4, s, s - second)
        joins = (part == 4) & (g > 1)
        own = list(range(pieces))
        for t in own:
            mine[t] = gathered[slot, t, me]

        @pl.when(joins)
        def _():
            pass_copy(last, me, 0).wait_recv()
            mine[last] = mine[last] + arriving[last, me]
            final[last] = mine[last]

        centre = []
        for r in range(3):
            every = sum(mine[t, b, r : r + 1, :] for t in own for b in range(some))
            centre.append(
                jnp.sum(every, keepdims=True) * (1.0 / (len(own) * some * BLOCK))
            )
        for t in own:
            target_features(t, centre)
            source_features(mine.at[t], t, me, centre)
        near = order[::-1]
        found = [partner]
        for d in near:
            found += [twin(d, -1), mirror(twin(d, -1))]
        for t in range(pieces):
            for p in found:
                copy(slot, t, p, p, 0).wait_recv()
                if t == last:

                    @pl.when(joins)
                    def _():
                        pass_copy(t, p, 0).wait_recv()
                        gathered[slot, t, p] = gathered[slot, t, p] + arriving[t, p]

                source_features(gathered.at[slot, t, p], t, p, centre)

        def finish(u, t):
            rates(u, t, centre)
            now = rate[u]
            current = mine[t]

            def put(value):
                gathered[other, t, me] = value

            @pl.when(part == 0)
            def _():
                base[t] = current
                f0[t] = now
                put(current + (0.5 * h) * now)

            @pl.when(part == 1)
            def _():
                f1[t] = now
                put(current + (0.5 * h) * now)

            @pl.when(part == 2)
            def _():
                f2[t] = now
                put(
                    base[t]
                    + h * (5.0 / 24.0 * f0[t] + 1.0 / 3.0 * f1[t] - 1.0 / 24.0 * now)
                )

            @pl.when(part == 3)
            def _():
                coarse = base[t] + h * f0[t]
                correction = (
                    current
                    + (0.5 * h) * (now - f1[t])
                    + h * (-1.0 / 24.0 * f0[t] + 1.0 / 3.0 * f1[t] + 5.0 / 24.0 * f2[t])
                    - coarse
                )

                @pl.when(s == 3)
                def _():
                    c0[t] = correction

                @pl.when((s > 3) & (g > 1) & (g < slices - 1))
                def _():
                    put(correction)

                @pl.when((s > 3) & (g > 1) & (g == slices - 1))
                def _():
                    final[t] = correction
                    if t == last:
                        for each in range(pieces):
                            pass_copy(each, me, 0).wait_recv()
                            final[each] = final[each] + arriving[each, me]

                @pl.when((s == 3) | (g <= 1))
                def _():
                    put(coarse + correction)
                    final[t] = coarse + correction

            @pl.when(part < 0)
            def _():
                put(current + h * now + c0[t])

            @pl.when(part == 4)
            def _():
                outgoing[t] = current + h * now
                pass_copy(t, me, 0).start()

                if t == last:

                    @pl.when(g < slices - 2)
                    def _():
                        for d in range(1, spaces):
                            pass_copy(t, me, d).start()

            meets = (part == 3) & (s > 3) & (g > 1)
            send_now = (s < steps - 1) if t == last else (s < steps - 1) & jnp.logical_not(meets)

            @pl.when(send_now)
            def _():
                for each in sends(other, t):
                    each.start()

            if t == last:

                @pl.when(meets & (s < steps - 1))
                def _():
                    for early in range(last):
                        pass_copy(early, me, 0).wait_recv()
                        value = gathered[other, early, me] + arriving[early, me]
                        gathered[other, early, me] = value
                        final[early] = value
                        for each in sends(other, early):
                            each.start()

        some_targets(list(range(pieces)), finish)
        for t in range(pieces):
            for each in sends(slot, t):
                each.wait_send()
        return carry

    lax.fori_loop(0, steps, step, 0)

    for t in range(pieces):
        for b in range(some):
            for r in range(6):
                at = r * blocks + t * some + b
                out_ref[at : at + 1, :] = final[t, b, r : r + 1, :]

    @pl.when((g > 0) & (g < slices - 1))
    def _():
        for t in range(pieces):
            pass_copy(t, me, 0).wait_send()

    @pl.when((g > 0) & (g < slices - 2))
    def _():
        for d in range(1, spaces):
            pass_copy(last, me, d).wait_send()


def per_device(spaces, slices, positions, strengths, source_lists, block_slot):
    blocks, width = source_lists.shape
    whole = block_slot.shape[0]
    pieces = 2 if blocks % 2 == 0 else 1
    tiles = (blocks // pieces, 6, BLOCK)
    state = pltpu.VMEM((pieces,) + tiles, jnp.float32)
    anywhere = pl.BlockSpec(memory_space=pl.ANY)
    out = pl.pallas_call(
        functools.partial(kernel, spaces, slices, blocks, width, pieces),
        out_shape=jax.ShapeDtypeStruct((6 * blocks, BLOCK), jnp.float32),
        in_specs=[anywhere] * 4,
        out_specs=pl.BlockSpec(memory_space=pltpu.VMEM),
        scratch_shapes=[
            pltpu.VMEM(positions.shape, jnp.float32),
            pltpu.VMEM(strengths.shape, jnp.float32),
            pltpu.SMEM(source_lists.shape, jnp.int32),
            pltpu.SMEM(block_slot.shape, jnp.int32),
            pltpu.VMEM((2, pieces, spaces) + tiles, jnp.float32),
            state,
            pltpu.VMEM((pieces,) + tiles, jnp.float32),
            state, state, state, state, state, state,
            pltpu.VMEM((pieces, spaces) + tiles, jnp.float32),
            state,
            pltpu.VMEM((blocks * TERMS, BLOCK), jnp.float32),
            pltpu.VMEM((whole, DEPTH, BLOCK), jnp.bfloat16),
            pltpu.VMEM((whole, PIECES * TERMS, BLOCK), jnp.bfloat16),
            pltpu.VMEM((blocks, BLOCK, DEPTH), jnp.bfloat16),
            pltpu.SemaphoreType.DMA((4,)),
            pltpu.SemaphoreType.DMA((2, pieces, spaces)),
            pltpu.SemaphoreType.DMA((2, pieces, spaces)),
            pltpu.SemaphoreType.DMA((pieces, spaces)),
            pltpu.SemaphoreType.DMA((pieces, spaces)),
        ],
        compiler_params=pltpu.CompilerParams(collective_id=0, has_side_effects=True),
    )(positions, strengths, source_lists, block_slot)
    return out.reshape(1, 6, blocks * BLOCK)


def solution(mesh):
    return jax.shard_map(
        functools.partial(per_device, mesh.shape["space"], mesh.shape["tm"]),
        mesh=mesh,
        in_specs=(P(None, "space"), P(None, "space"), P("space", None), P()),
        out_specs=P("tm", None, "space"),
        check_vma=False,
    )
```

```python
import functools

import jax
import jax.numpy as jnp
from jax import lax
from jax.experimental import pallas as pl
from jax.experimental.pallas import tpu as pltpu
from jax.sharding import PartitionSpec as P

BLOCK = 128
SUB = 8
PIECES = 3
TERMS = 32
DEPTH = 32
AHEAD = 6
MESH = pl.DeviceIdType.MESH

time_step = 0.1
core_square = 0.25
inv_four_pi = 0.07957747154594767


def cross(u, v):
    return [
        u[1] * v[2] - u[2] * v[1],
        u[2] * v[0] - u[0] * v[2],
        u[0] * v[1] - u[1] * v[0],
    ]


def dot3(u, v):
    return u[0] * v[0] + u[1] * v[1] + u[2] * v[2]


def rounded(v):
    return v.astype(jnp.bfloat16).astype(jnp.float32)


def split3(v):
    high = rounded(v)
    rest = v - high
    middle = rounded(rest)
    return high, middle, rounded(rest - middle)


def kernel(
    spaces, slices, blocks, width, pieces,
    pos_hbm, str_hbm, list_hbm, slot_hbm, out_ref,
    pos_ref, str_ref, list_ref, slot_ref,
    gathered, mine, rate, final, base, f0, f1, f2, c0, arriving, outgoing,
    sums, feat, moment, coef, load_sem, send_sem, recv_sem, give_sem, take_sem,
):
    me = lax.axis_index("space")
    g = lax.axis_index("tm")
    h = time_step
    some = blocks // pieces
    last = pieces - 1

    loads = [
        pltpu.make_async_copy(src, dst, load_sem.at[k])
        for k, (src, dst) in enumerate(
            [(pos_hbm, pos_ref), (str_hbm, str_ref), (list_hbm, list_ref), (slot_hbm, slot_ref)]
        )
    ]
    for each in loads:
        each.start()

    barrier = pltpu.get_barrier_semaphore()

    def greet(d, carry):
        peer = lax.rem(me + d, spaces)
        pl.semaphore_signal(barrier, inc=1, device_id={"space": peer}, device_id_type=MESH)
        return carry

    lax.fori_loop(1, spaces, greet, 0)

    def greet_before(d, carry):
        peer = lax.rem(me + d, spaces)
        pl.semaphore_signal(
            barrier, inc=1, device_id={"space": peer, "tm": g - 1}, device_id_type=MESH
        )
        return carry

    @pl.when((g > 1) & (g < slices - 1))
    def _():
        lax.fori_loop(0, spaces, greet_before, 0)

    @pl.when((g > 1) & (g == slices - 1))
    def _():
        greet_before(0, 0)

    for each in loads:
        each.wait()

    for b in range(blocks):
        cols = slice(b * BLOCK, (b + 1) * BLOCK)
        piece, at = divmod(b, some)
        for r in range(3):
            gathered[0, piece, me, at, r : r + 1, :] = pos_ref[r : r + 1, cols]
            gathered[0, piece, me, at, 3 + r : 4 + r, :] = str_ref[r : r + 1, cols]

    after = jnp.where(g < slices - 2, spaces, jnp.where(g < slices - 1, 1, 0))
    pl.semaphore_wait(barrier, spaces - 1 + jnp.where(g > 0, after, 0))

    chips = spaces // 2
    tall = chips // 2
    core = lax.rem(me, 2)
    column = lax.rem(me // 2, 2)
    row = me // 4
    partner = me + 1 - 2 * core

    def twin(d, sign):
        other_column = lax.rem(column + d % 2, 2)
        other_row = lax.rem(row + tall + sign * (d // 2), tall)
        return 2 * (2 * other_row + other_column) + core

    def copy(slot, t, what, where, sem):
        return pltpu.make_async_remote_copy(
            src_ref=gathered.at[slot, t, what],
            dst_ref=gathered.at[slot, t, what],
            send_sem=send_sem.at[slot, t, sem],
            recv_sem=recv_sem.at[slot, t, what],
            device_id={"space": where},
            device_id_type=MESH,
        )

    order = sorted(range(1, chips), key=lambda d: (-(d % 2) - (d // 2), d))

    def mirror(p):
        return p + 1 - 2 * core

    def sends(slot, t):
        found = []
        for d in order:
            found.append(copy(slot, t, me, twin(d, 1), d))
            found.append(copy(slot, t, me, mirror(twin(d, 1)), chips + d))
        return found + [copy(slot, t, me, partner, 0)]

    def pass_copy(t, what, d):
        return pltpu.make_async_remote_copy(
            src_ref=outgoing.at[t],
            dst_ref=arriving.at[t, what],
            send_sem=give_sem.at[t, d],
            recv_sem=take_sem.at[t, what],
            device_id={"space": lax.rem(me + d, spaces), "tm": lax.rem(g + 1, slices)},
            device_id_type=MESH,
        )

    at_row = lax.broadcasted_iota(jnp.int32, (SUB, BLOCK), 0)

    def stack(values):
        found = values[0]
        for r, v in enumerate(values[1:]):
            found = jnp.where(at_row > r, v, found)
        return found

    def spread(v):
        return jnp.broadcast_to(v, (SUB, BLOCK))

    def source_block(tile, t, p, b, centre):
        rows = [tile[b, r : r + 1, :] for r in range(6)]
        x = [spread(v) - c for v, c in zip(rows[:3], centre)]
        a = [spread(v) for v in rows[3:]]
        square = dot3(x, x)
        six = a + cross(x, a)
        whole = stack([x[0], x[1], x[2], square, jnp.ones_like(square), x[0], x[1], x[2]])
        high, middle, low = split3(whole)
        second = jnp.where((at_row <= 2) | (at_row == 4), high, middle)
        third = jnp.where(at_row == 4, high, jnp.where(at_row <= 2, middle, low))
        at = p * blocks + t * some + b
        feat[at] = jnp.concatenate(
            [high, second, third, jnp.zeros_like(high)], 0
        ).astype(jnp.bfloat16)
        common = stack(six)
        inner = at_row <= 5
        parts = []
        for k in range(3):
            ends = jnp.where(at_row == 6, six[2 * k], six[2 * k + 1])
            parts.append(jnp.where(inner, common * x[k], ends))
        parts.append(common * square)
        pieces = split3(jnp.concatenate(parts, 0))
        moment[at] = jnp.concatenate(pieces, 0).astype(jnp.bfloat16)

    def source_features(tile, t, p, centre):
        for b in range(some):
            source_block(tile, t, p, b, centre)

    def target_features(t, centre):
        for b in range(some):
            x = [spread(mine[t, b, r : r + 1, :]) - centre[r] for r in range(3)]
            square = dot3(x, x) + core_square
            minus = [-2.0 * v for v in x]
            high, middle, low = split3(
                stack(minus + [jnp.ones_like(square), square] + minus)
            )
            first = jnp.where(at_row <= 4, high, middle)
            exact = (at_row == 3) | (at_row >= 5)
            second = jnp.where(exact, high, jnp.where(at_row == 4, middle, low))
            third = jnp.where(exact, high, jnp.where(at_row == 4, low, middle))
            rows = jnp.concatenate([first, second, third, jnp.zeros_like(first)], 0)
            coef[t * some + b] = rows.T.astype(jnp.bfloat16)

    group = 2 if width % 2 == 0 else 1

    def pair_product(i, j):
        at = [slot_ref[list_ref[i, j + k]] for k in range(group)]
        right = jnp.concatenate([feat[p] for p in at], 1)
        both = lax.dot_general(
            coef[i], right, (((1,), (0,)), ((), ())), preferred_element_type=jnp.float32
        )
        return at, both

    def pair_sums(at, both):
        inverse = lax.rsqrt(both)
        square = inverse * inverse
        weight = (square * square) * inverse
        high = weight.astype(jnp.bfloat16)
        low = (weight - high.astype(jnp.float32)).astype(jnp.bfloat16)
        moments = jnp.concatenate([moment[p] for p in at], 1)
        rows = (((1,), (1,)), ((), ()))
        first = jnp.concatenate([moment[p, :TERMS] for p in at], 1)
        return (
            lax.dot_general(moments, high, rows, preferred_element_type=jnp.float32),
            lax.dot_general(first, low, rows, preferred_element_type=jnp.float32),
        )

    def some_targets(chosen, finish):
        work = [(n, j) for n in range(len(chosen) * some) for j in range(0, width, group)]
        waiting = []
        total, small = 0.0, 0.0
        for k in range(len(work) + AHEAD):
            if k < len(work):
                n, j = work[k]
                waiting.append((n, pair_product(chosen[n // some] * some + n % some, j)))
            if k >= AHEAD:
                n, (at, both) = waiting.pop(0)
                large_part, small_part = pair_sums(at, both)
                total += large_part
                small += small_part
                if k - AHEAD == len(work) - 1 or work[k - AHEAD + 1][0] != n:
                    sums[n * TERMS : (n + 1) * TERMS, :] = (
                        (total[2 * TERMS :] + small) + total[TERMS : 2 * TERMS] + total[:TERMS]
                    )
                    total, small = 0.0, 0.0
                    if (n + 1) % some == 0:
                        finish(n // some, chosen[n // some])

    def rates(u, t, centre):
        row = lambda r: jnp.concatenate([mine[t, b, r : r + 1, :] for b in range(some)], 0)
        x = [row(r) - centre[r] for r in range(3)]
        a = [row(3 + r) for r in range(3)]
        pick = lambda r: sums[pl.ds(u * some * TERMS + r, some, stride=TERMS), :]
        plain = [pick(SUB * (c // 2) + 6 + c % 2) for c in range(6)]
        along = [[pick(SUB * k + c) for c in range(6)] for k in range(3)]
        squared = [pick(SUB * 3 + c) for c in range(6)]
        near = dot3(x, x) + core_square
        turn = dot3(a, x)
        three = [
            near * plain[c] - 2.0 * dot3(x, [along[k][c] for k in range(3)]) + squared[c]
            for c in range(6)
        ]
        five = [
            turn * plain[c] - dot3(a, [along[k][c] for k in range(3)]) for c in range(6)
        ]
        cross_v = cross(x, three[:3])
        cross_s = cross(a, three[:3])
        cross_f = cross(x, five[:3])
        velocity = [-inv_four_pi * (cross_v[r] - three[3 + r]) for r in range(3)]
        stretch = [
            -inv_four_pi * (cross_s[r] - 3.0 * (cross_f[r] - five[3 + r])) for r in range(3)
        ]
        for r, v in enumerate(velocity + stretch):
            for b in range(some):
                rate[u, b, r : r + 1, :] = v[b : b + 1, :]

    second = 3 + g
    steps = jnp.where(g == 0, 4, jnp.where(g < slices - 1, g + 8, g + 7))

    for t in range(pieces):
        for each in sends(0, t):
            each.start()

    def step(s, carry):
        slot = lax.rem(s, 2)
        other = 1 - slot
        part = jnp.where(s < 4, s, s - second)
        joins = (part == 4) & (g > 1)
        own = list(range(pieces))
        for t in own:
            mine[t] = gathered[slot, t, me]

        @pl.when(joins)
        def _():
            pass_copy(last, me, 0).wait_recv()
            mine[last] = mine[last] + arriving[last, me]
            final[last] = mine[last]

        centre = []
        for r in range(3):
            every = sum(mine[t, b, r : r + 1, :] for t in own for b in range(some))
            centre.append(
                jnp.sum(every, keepdims=True) * (1.0 / (len(own) * some * BLOCK))
            )
        for t in own:
            target_features(t, centre)
            source_features(mine.at[t], t, me, centre)
        near = order[::-1]
        found = [partner]
        for d in near:
            found += [twin(d, -1), mirror(twin(d, -1))]
        for t in range(pieces):
            for p in found:
                copy(slot, t, p, p, 0).wait_recv()
                if t == last:

                    @pl.when(joins)
                    def _():
                        pass_copy(t, p, 0).wait_recv()
                        gathered[slot, t, p] = gathered[slot, t, p] + arriving[t, p]

                source_features(gathered.at[slot, t, p], t, p, centre)

        def finish(u, t):
            rates(u, t, centre)
            now = rate[u]
            current = mine[t]

            def put(value):
                gathered[other, t, me] = value

            @pl.when(part == 0)
            def _():
                base[t] = current
                f0[t] = now
                put(current + (0.5 * h) * now)

            @pl.when(part == 1)
            def _():
                f1[t] = now
                put(current + (0.5 * h) * now)

            @pl.when(part == 2)
            def _():
                f2[t] = now
                put(
                    base[t]
                    + h * (5.0 / 24.0 * f0[t] + 1.0 / 3.0 * f1[t] - 1.0 / 24.0 * now)
                )

            @pl.when(part == 3)
            def _():
                coarse = base[t] + h * f0[t]
                correction = (
                    current
                    + (0.5 * h) * (now - f1[t])
                    + h * (-1.0 / 24.0 * f0[t] + 1.0 / 3.0 * f1[t] + 5.0 / 24.0 * f2[t])
                    - coarse
                )

                @pl.when(s == 3)
                def _():
                    c0[t] = correction

                @pl.when((s > 3) & (g > 1) & (g < slices - 1))
                def _():
                    put(correction)

                @pl.when((s > 3) & (g > 1) & (g == slices - 1))
                def _():
                    final[t] = correction
                    if t == last:
                        for each in range(pieces):
                            pass_copy(each, me, 0).wait_recv()
                            final[each] = final[each] + arriving[each, me]

                @pl.when((s == 3) | (g <= 1))
                def _():
                    put(coarse + correction)
                    final[t] = coarse + correction

            @pl.when(part < 0)
            def _():
                put(current + h * now + c0[t])

            @pl.when(part == 4)
            def _():
                outgoing[t] = current + h * now
                pass_copy(t, me, 0).start()

                if t == last:

                    @pl.when(g < slices - 2)
                    def _():
                        for d in range(1, spaces):
                            pass_copy(t, me, d).start()

            meets = (part == 3) & (s > 3) & (g > 1)
            send_now = (s < steps - 1) if t == last else (s < steps - 1) & jnp.logical_not(meets)

            @pl.when(send_now)
            def _():
                for each in sends(other, t):
                    each.start()

            if t == last:

                @pl.when(meets & (s < steps - 1))
                def _():
                    for early in range(last):
                        pass_copy(early, me, 0).wait_recv()
                        value = gathered[other, early, me] + arriving[early, me]
                        gathered[other, early, me] = value
                        final[early] = value
                        for each in sends(other, early):
                            each.start()

        some_targets(list(range(pieces)), finish)
        for t in range(pieces):
            for each in sends(slot, t):
                each.wait_send()
        return carry

    lax.fori_loop(0, steps, step, 0)

    for t in range(pieces):
        for b in range(some):
            for r in range(6):
                at = r * blocks + t * some + b
                out_ref[at : at + 1, :] = final[t, b, r : r + 1, :]

    @pl.when((g > 0) & (g < slices - 1))
    def _():
        for t in range(pieces):
            pass_copy(t, me, 0).wait_send()

    @pl.when((g > 0) & (g < slices - 2))
    def _():
        for d in range(1, spaces):
            pass_copy(last, me, d).wait_send()


def per_device(spaces, slices, positions, strengths, source_lists, block_slot):
    blocks, width = source_lists.shape
    whole = block_slot.shape[0]
    pieces = 2 if blocks % 2 == 0 else 1
    tiles = (blocks // pieces, 6, BLOCK)
    state = pltpu.VMEM((pieces,) + tiles, jnp.float32)
    anywhere = pl.BlockSpec(memory_space=pl.ANY)
    out = pl.pallas_call(
        functools.partial(kernel, spaces, slices, blocks, width, pieces),
        out_shape=jax.ShapeDtypeStruct((6 * blocks, BLOCK), jnp.float32),
        in_specs=[anywhere] * 4,
        out_specs=pl.BlockSpec(memory_space=pltpu.VMEM),
        scratch_shapes=[
            pltpu.VMEM(positions.shape, jnp.float32),
            pltpu.VMEM(strengths.shape, jnp.float32),
            pltpu.SMEM(source_lists.shape, jnp.int32),
            pltpu.SMEM(block_slot.shape, jnp.int32),
            pltpu.VMEM((2, pieces, spaces) + tiles, jnp.float32),
            state,
            pltpu.VMEM((pieces,) + tiles, jnp.float32),
            state, state, state, state, state, state,
            pltpu.VMEM((pieces, spaces) + tiles, jnp.float32),
            state,
            pltpu.VMEM((blocks * TERMS, BLOCK), jnp.float32),
            pltpu.VMEM((whole, DEPTH, BLOCK), jnp.bfloat16),
            pltpu.VMEM((whole, PIECES * TERMS, BLOCK), jnp.bfloat16),
            pltpu.VMEM((blocks, BLOCK, DEPTH), jnp.bfloat16),
            pltpu.SemaphoreType.DMA((4,)),
            pltpu.SemaphoreType.DMA((2, pieces, spaces)),
            pltpu.SemaphoreType.DMA((2, pieces, spaces)),
            pltpu.SemaphoreType.DMA((pieces, spaces)),
            pltpu.SemaphoreType.DMA((pieces, spaces)),
        ],
        compiler_params=pltpu.CompilerParams(collective_id=0, has_side_effects=True),
    )(positions, strengths, source_lists, block_slot)
    return out.reshape(1, 6, blocks * BLOCK)


def solution(mesh):
    return jax.shard_map(
        functools.partial(per_device, mesh.shape["space"], mesh.shape["tm"]),
        mesh=mesh,
        in_specs=(P(None, "space"), P(None, "space"), P("space", None), P()),
        out_specs=P("tm", None, "space"),
        check_vma=False,
    )
```

```python
import functools

import jax
import jax.numpy as jnp
from jax import lax
from jax.experimental import pallas as pl
from jax.experimental.pallas import tpu as pltpu
from jax.sharding import PartitionSpec as P

BLOCK = 128
SUB = 8
PIECES = 3
TERMS = 32
DEPTH = 32
AHEAD = 6
MESH = pl.DeviceIdType.MESH

time_step = 0.1
core_square = 0.25
inv_four_pi = 0.07957747154594767


def cross(u, v):
    return [
        u[1] * v[2] - u[2] * v[1],
        u[2] * v[0] - u[0] * v[2],
        u[0] * v[1] - u[1] * v[0],
    ]


def dot3(u, v):
    return u[0] * v[0] + u[1] * v[1] + u[2] * v[2]


def rounded(v):
    return v.astype(jnp.bfloat16).astype(jnp.float32)


def split3(v):
    high = rounded(v)
    rest = v - high
    middle = rounded(rest)
    return high, middle, rounded(rest - middle)


def kernel(
    spaces, slices, blocks, width, pieces,
    pos_hbm, str_hbm, list_hbm, slot_hbm, out_ref,
    pos_ref, str_ref, list_ref, slot_ref,
    gathered, mine, rate, final, base, f0, f1, f2, c0, arriving, outgoing,
    sums, feat, moment, coef, load_sem, send_sem, recv_sem, give_sem, take_sem,
):
    me = lax.axis_index("space")
    g = lax.axis_index("tm")
    h = time_step
    some = blocks // pieces
    last = pieces - 1

    loads = [
        pltpu.make_async_copy(src, dst, load_sem.at[k])
        for k, (src, dst) in enumerate(
            [(pos_hbm, pos_ref), (str_hbm, str_ref), (list_hbm, list_ref), (slot_hbm, slot_ref)]
        )
    ]
    for each in loads:
        each.start()

    barrier = pltpu.get_barrier_semaphore()

    def greet(d, carry):
        peer = lax.rem(me + d, spaces)
        pl.semaphore_signal(barrier, inc=1, device_id={"space": peer}, device_id_type=MESH)
        return carry

    lax.fori_loop(1, spaces, greet, 0)

    def greet_before(d, carry):
        peer = lax.rem(me + d, spaces)
        pl.semaphore_signal(
            barrier, inc=1, device_id={"space": peer, "tm": g - 1}, device_id_type=MESH
        )
        return carry

    @pl.when((g > 1) & (g < slices - 1))
    def _():
        lax.fori_loop(0, spaces, greet_before, 0)

    @pl.when((g > 1) & (g == slices - 1))
    def _():
        greet_before(0, 0)

    for each in loads:
        each.wait()

    for b in range(blocks):
        cols = slice(b * BLOCK, (b + 1) * BLOCK)
        piece, at = divmod(b, some)
        for r in range(3):
            gathered[0, piece, me, at, r : r + 1, :] = pos_ref[r : r + 1, cols]
            gathered[0, piece, me, at, 3 + r : 4 + r, :] = str_ref[r : r + 1, cols]

    after = jnp.where(g < slices - 2, spaces, jnp.where(g < slices - 1, 1, 0))
    pl.semaphore_wait(barrier, spaces - 1 + jnp.where(g > 0, after, 0))

    chips = spaces // 2
    tall = chips // 2
    core = lax.rem(me, 2)
    column = lax.rem(me // 2, 2)
    row = me // 4
    partner = me + 1 - 2 * core

    def twin(d, sign):
        other_column = lax.rem(column + d % 2, 2)
        other_row = lax.rem(row + tall + sign * (d // 2), tall)
        return 2 * (2 * other_row + other_column) + core

    def copy(slot, t, what, where, sem):
        return pltpu.make_async_remote_copy(
            src_ref=gathered.at[slot, t, what],
            dst_ref=gathered.at[slot, t, what],
            send_sem=send_sem.at[slot, t, sem],
            recv_sem=recv_sem.at[slot, t, what],
            device_id={"space": where},
            device_id_type=MESH,
        )

    order = sorted(range(1, chips), key=lambda d: (-(d % 2) - (d // 2), d))

    def mirror(p):
        return p + 1 - 2 * core

    def sends(slot, t):
        found = []
        for d in order:
            found.append(copy(slot, t, me, twin(d, 1), d))
            found.append(copy(slot, t, me, mirror(twin(d, 1)), chips + d))
        return found + [copy(slot, t, me, partner, 0)]

    def pass_copy(t, what, d):
        return pltpu.make_async_remote_copy(
            src_ref=outgoing.at[t],
            dst_ref=arriving.at[t, what],
            send_sem=give_sem.at[t, d],
            recv_sem=take_sem.at[t, what],
            device_id={"space": lax.rem(me + d, spaces), "tm": lax.rem(g + 1, slices)},
            device_id_type=MESH,
        )

    at_row = lax.broadcasted_iota(jnp.int32, (SUB, BLOCK), 0)

    def stack(values):
        found = values[0]
        for r, v in enumerate(values[1:]):
            found = jnp.where(at_row > r, v, found)
        return found

    def spread(v):
        return jnp.broadcast_to(v, (SUB, BLOCK))

    def source_block(tile, t, p, b, centre):
        rows = [tile[b, r : r + 1, :] for r in range(6)]
        x = [spread(v) - c for v, c in zip(rows[:3], centre)]
        a = [spread(v) for v in rows[3:]]
        square = dot3(x, x)
        six = a + cross(x, a)
        whole = stack([x[0], x[1], x[2], square, jnp.ones_like(square), x[0], x[1], x[2]])
        high, middle, low = split3(whole)
        second = jnp.where((at_row <= 2) | (at_row == 4), high, middle)
        third = jnp.where(at_row == 4, high, jnp.where(at_row <= 2, middle, low))
        at = p * blocks + t * some + b
        feat[at] = jnp.concatenate(
            [high, second, third, jnp.zeros_like(high)], 0
        ).astype(jnp.bfloat16)
        common = stack(six)
        inner = at_row <= 5
        parts = []
        for k in range(3):
            ends = jnp.where(at_row == 6, six[2 * k], six[2 * k + 1])
            parts.append(jnp.where(inner, common * x[k], ends))
        parts.append(common * square)
        pieces = split3(jnp.concatenate(parts, 0))
        moment[at] = jnp.concatenate(pieces, 0).astype(jnp.bfloat16)

    def source_features(tile, t, p, centre):
        for b in range(some):
            source_block(tile, t, p, b, centre)

    def target_features(t, centre):
        for b in range(some):
            x = [spread(mine[t, b, r : r + 1, :]) - centre[r] for r in range(3)]
            square = dot3(x, x) + core_square
            minus = [-2.0 * v for v in x]
            high, middle, low = split3(
                stack(minus + [jnp.ones_like(square), square] + minus)
            )
            first = jnp.where(at_row <= 4, high, middle)
            exact = (at_row == 3) | (at_row >= 5)
            second = jnp.where(exact, high, jnp.where(at_row == 4, middle, low))
            third = jnp.where(exact, high, jnp.where(at_row == 4, low, middle))
            rows = jnp.concatenate([first, second, third, jnp.zeros_like(first)], 0)
            coef[t * some + b] = rows.T.astype(jnp.bfloat16)

    group = 2 if width % 2 == 0 else 1

    def pair_product(i, j):
        at = [slot_ref[list_ref[i, j + k]] for k in range(group)]
        right = jnp.concatenate([feat[p] for p in at], 1)
        both = lax.dot_general(
            coef[i], right, (((1,), (0,)), ((), ())), preferred_element_type=jnp.float32
        )
        return at, both

    def pair_sums(at, both):
        inverse = lax.rsqrt(both)
        square = inverse * inverse
        weight = (square * square) * inverse
        high = weight.astype(jnp.bfloat16)
        low = (weight - high.astype(jnp.float32)).astype(jnp.bfloat16)
        moments = jnp.concatenate([moment[p] for p in at], 1)
        rows = (((1,), (1,)), ((), ()))
        return lax.dot_general(
            moments, high, rows, preferred_element_type=jnp.float32
        ) + lax.dot_general(moments, low, rows, preferred_element_type=jnp.float32)

    def some_targets(chosen, finish):
        work = [(n, j) for n in range(len(chosen) * some) for j in range(0, width, group)]
        waiting = []
        total = 0.0
        for k in range(len(work) + AHEAD):
            if k < len(work):
                n, j = work[k]
                waiting.append((n, pair_product(chosen[n // some] * some + n % some, j)))
            if k >= AHEAD:
                n, (at, both) = waiting.pop(0)
                total += pair_sums(at, both)
                if k - AHEAD == len(work) - 1 or work[k - AHEAD + 1][0] != n:
                    sums[n * TERMS : (n + 1) * TERMS, :] = (
                        total[2 * TERMS :] + total[TERMS : 2 * TERMS] + total[:TERMS]
                    )
                    total = 0.0
                    if (n + 1) % some == 0:
                        finish(n // some, chosen[n // some])

    def rates(u, t, centre):
        row = lambda r: jnp.concatenate([mine[t, b, r : r + 1, :] for b in range(some)], 0)
        x = [row(r) - centre[r] for r in range(3)]
        a = [row(3 + r) for r in range(3)]
        pick = lambda r: sums[pl.ds(u * some * TERMS + r, some, stride=TERMS), :]
        plain = [pick(SUB * (c // 2) + 6 + c % 2) for c in range(6)]
        along = [[pick(SUB * k + c) for c in range(6)] for k in range(3)]
        squared = [pick(SUB * 3 + c) for c in range(6)]
        near = dot3(x, x) + core_square
        turn = dot3(a, x)
        three = [
            near * plain[c] - 2.0 * dot3(x, [along[k][c] for k in range(3)]) + squared[c]
            for c in range(6)
        ]
        five = [
            turn * plain[c] - dot3(a, [along[k][c] for k in range(3)]) for c in range(6)
        ]
        cross_v = cross(x, three[:3])
        cross_s = cross(a, three[:3])
        cross_f = cross(x, five[:3])
        velocity = [-inv_four_pi * (cross_v[r] - three[3 + r]) for r in range(3)]
        stretch = [
            -inv_four_pi * (cross_s[r] - 3.0 * (cross_f[r] - five[3 + r])) for r in range(3)
        ]
        for r, v in enumerate(velocity + stretch):
            for b in range(some):
                rate[u, b, r : r + 1, :] = v[b : b + 1, :]

    second = 3 + g
    steps = jnp.where(g == 0, 4, jnp.where(g < slices - 1, g + 8, g + 7))

    for t in range(pieces):
        for each in sends(0, t):
            each.start()

    def step(s, carry):
        slot = lax.rem(s, 2)
        other = 1 - slot
        part = jnp.where(s < 4, s, s - second)
        joins = (part == 4) & (g > 1)
        own = list(range(pieces))
        for t in own:
            mine[t] = gathered[slot, t, me]

        @pl.when(joins)
        def _():
            pass_copy(last, me, 0).wait_recv()
            mine[last] = mine[last] + arriving[last, me]
            final[last] = mine[last]

        centre = []
        for r in range(3):
            every = sum(mine[t, b, r : r + 1, :] for t in own for b in range(some))
            centre.append(
                jnp.sum(every, keepdims=True) * (1.0 / (len(own) * some * BLOCK))
            )
        for t in own:
            target_features(t, centre)
            source_features(mine.at[t], t, me, centre)
        near = order[::-1]
        found = [partner]
        for d in near:
            found += [twin(d, -1), mirror(twin(d, -1))]
        for t in range(pieces):
            for p in found:
                copy(slot, t, p, p, 0).wait_recv()
                if t == last:

                    @pl.when(joins)
                    def _():
                        pass_copy(t, p, 0).wait_recv()
                        gathered[slot, t, p] = gathered[slot, t, p] + arriving[t, p]

                source_features(gathered.at[slot, t, p], t, p, centre)

        def finish(u, t):
            rates(u, t, centre)
            now = rate[u]
            current = mine[t]

            def put(value):
                gathered[other, t, me] = value

            @pl.when(part == 0)
            def _():
                base[t] = current
                f0[t] = now
                put(current + (0.5 * h) * now)

            @pl.when(part == 1)
            def _():
                f1[t] = now
                put(current + (0.5 * h) * now)

            @pl.when(part == 2)
            def _():
                f2[t] = now
                put(
                    base[t]
                    + h * (5.0 / 24.0 * f0[t] + 1.0 / 3.0 * f1[t] - 1.0 / 24.0 * now)
                )

            @pl.when(part == 3)
            def _():
                coarse = base[t] + h * f0[t]
                correction = (
                    current
                    + (0.5 * h) * (now - f1[t])
                    + h * (-1.0 / 24.0 * f0[t] + 1.0 / 3.0 * f1[t] + 5.0 / 24.0 * f2[t])
                    - coarse
                )

                @pl.when(s == 3)
                def _():
                    c0[t] = correction

                @pl.when((s > 3) & (g > 1) & (g < slices - 1))
                def _():
                    put(correction)

                @pl.when((s > 3) & (g > 1) & (g == slices - 1))
                def _():
                    final[t] = correction
                    if t == last:
                        for each in range(pieces):
                            pass_copy(each, me, 0).wait_recv()
                            final[each] = final[each] + arriving[each, me]

                @pl.when((s == 3) | (g <= 1))
                def _():
                    put(coarse + correction)
                    final[t] = coarse + correction

            @pl.when(part < 0)
            def _():
                put(current + h * now + c0[t])

            @pl.when(part == 4)
            def _():
                outgoing[t] = current + h * now
                pass_copy(t, me, 0).start()

                if t == last:

                    @pl.when(g < slices - 2)
                    def _():
                        for d in range(1, spaces):
                            pass_copy(t, me, d).start()

            meets = (part == 3) & (s > 3) & (g > 1)
            send_now = (s < steps - 1) if t == last else (s < steps - 1) & jnp.logical_not(meets)

            @pl.when(send_now)
            def _():
                for each in sends(other, t):
                    each.start()

            if t == last:

                @pl.when(meets & (s < steps - 1))
                def _():
                    for early in range(last):
                        pass_copy(early, me, 0).wait_recv()
                        value = gathered[other, early, me] + arriving[early, me]
                        gathered[other, early, me] = value
                        final[early] = value
                        for each in sends(other, early):
                            each.start()

        some_targets(list(range(pieces)), finish)
        for t in range(pieces):
            for each in sends(slot, t):
                each.wait_send()
        return carry

    lax.fori_loop(0, steps, step, 0)

    for t in range(pieces):
        for b in range(some):
            for r in range(6):
                at = r * blocks + t * some + b
                out_ref[at : at + 1, :] = final[t, b, r : r + 1, :]

    @pl.when((g > 0) & (g < slices - 1))
    def _():
        for t in range(pieces):
            pass_copy(t, me, 0).wait_send()

    @pl.when((g > 0) & (g < slices - 2))
    def _():
        for d in range(1, spaces):
            pass_copy(last, me, d).wait_send()


def hand_out(from_ref, to_ref, sem):
    moved = pltpu.make_async_copy(from_ref, to_ref, sem)
    moved.start()
    moved.wait()


def per_device(spaces, slices, positions, strengths, source_lists, block_slot):
    blocks, width = source_lists.shape
    whole = block_slot.shape[0]
    pieces = 2 if blocks % 2 == 0 else 1
    tiles = (blocks // pieces, 6, BLOCK)
    state = pltpu.VMEM((pieces,) + tiles, jnp.float32)
    anywhere = pl.BlockSpec(memory_space=pl.ANY)
    out = pl.pallas_call(
        functools.partial(kernel, spaces, slices, blocks, width, pieces),
        out_shape=jax.ShapeDtypeStruct((6 * blocks, BLOCK), jnp.float32),
        in_specs=[anywhere] * 4,
        out_specs=pl.BlockSpec(memory_space=pltpu.VMEM),
        scratch_shapes=[
            pltpu.VMEM(positions.shape, jnp.float32),
            pltpu.VMEM(strengths.shape, jnp.float32),
            pltpu.SMEM(source_lists.shape, jnp.int32),
            pltpu.SMEM(block_slot.shape, jnp.int32),
            pltpu.VMEM((2, pieces, spaces) + tiles, jnp.float32),
            state,
            pltpu.VMEM((pieces,) + tiles, jnp.float32),
            state, state, state, state, state, state,
            pltpu.VMEM((pieces, spaces) + tiles, jnp.float32),
            state,
            pltpu.VMEM((blocks * TERMS, BLOCK), jnp.float32),
            pltpu.VMEM((whole, DEPTH, BLOCK), jnp.bfloat16),
            pltpu.VMEM((whole, PIECES * TERMS, BLOCK), jnp.bfloat16),
            pltpu.VMEM((blocks, BLOCK, DEPTH), jnp.bfloat16),
            pltpu.SemaphoreType.DMA((4,)),
            pltpu.SemaphoreType.DMA((2, pieces, spaces)),
            pltpu.SemaphoreType.DMA((2, pieces, spaces)),
            pltpu.SemaphoreType.DMA((pieces, spaces)),
            pltpu.SemaphoreType.DMA((pieces, spaces)),
        ],
        compiler_params=pltpu.CompilerParams(collective_id=0, has_side_effects=True),
    )(positions, strengths, source_lists, block_slot)
    out = pl.pallas_call(
        hand_out,
        out_shape=jax.ShapeDtypeStruct(out.shape, out.dtype),
        in_specs=[anywhere],
        out_specs=anywhere,
        scratch_shapes=[pltpu.SemaphoreType.DMA],
    )(out)
    return out.reshape(1, 6, blocks * BLOCK)


def solution(mesh):
    return jax.shard_map(
        functools.partial(per_device, mesh.shape["space"], mesh.shape["tm"]),
        mesh=mesh,
        in_specs=(P(None, "space"), P(None, "space"), P("space", None), P()),
        out_specs=P("tm", None, "space"),
        check_vma=False,
    )
```

```python
import functools

import jax
import jax.numpy as jnp
from jax import lax
from jax.experimental import pallas as pl
from jax.experimental.pallas import tpu as pltpu
from jax.sharding import PartitionSpec as P

BLOCK = 128
SUB = 8
PIECES = 3
TERMS = 32
DEPTH = 32
AHEAD = 3
MESH = pl.DeviceIdType.MESH

time_step = 0.1
core_square = 0.25
inv_four_pi = 0.07957747154594767


def cross(u, v):
    return [
        u[1] * v[2] - u[2] * v[1],
        u[2] * v[0] - u[0] * v[2],
        u[0] * v[1] - u[1] * v[0],
    ]


def dot3(u, v):
    return u[0] * v[0] + u[1] * v[1] + u[2] * v[2]


def rounded(v):
    return v.astype(jnp.bfloat16).astype(jnp.float32)


def split3(v):
    high = rounded(v)
    rest = v - high
    middle = rounded(rest)
    return high, middle, rounded(rest - middle)


def kernel(
    spaces, slices, blocks, width, pieces,
    pos_hbm, str_hbm, list_hbm, slot_hbm, out_ref,
    pos_ref, str_ref, list_ref, slot_ref,
    gathered, mine, rate, final, base, f0, f1, f2, c0, arriving, outgoing,
    sums, feat, moment, coef, load_sem, send_sem, recv_sem, give_sem, take_sem,
):
    me = lax.axis_index("space")
    g = lax.axis_index("tm")
    h = time_step
    some = blocks // pieces
    last = pieces - 1

    loads = [
        pltpu.make_async_copy(src, dst, load_sem.at[k])
        for k, (src, dst) in enumerate(
            [(pos_hbm, pos_ref), (str_hbm, str_ref), (list_hbm, list_ref), (slot_hbm, slot_ref)]
        )
    ]
    for each in loads:
        each.start()

    barrier = pltpu.get_barrier_semaphore()

    def greet(d, carry):
        peer = lax.rem(me + d, spaces)
        pl.semaphore_signal(barrier, inc=1, device_id={"space": peer}, device_id_type=MESH)
        return carry

    lax.fori_loop(1, spaces, greet, 0)

    def greet_before(d, carry):
        peer = lax.rem(me + d, spaces)
        pl.semaphore_signal(
            barrier, inc=1, device_id={"space": peer, "tm": g - 1}, device_id_type=MESH
        )
        return carry

    @pl.when((g > 1) & (g < slices - 1))
    def _():
        lax.fori_loop(0, spaces, greet_before, 0)

    @pl.when((g > 1) & (g == slices - 1))
    def _():
        greet_before(0, 0)

    for each in loads:
        each.wait()

    for b in range(blocks):
        cols = slice(b * BLOCK, (b + 1) * BLOCK)
        piece, at = divmod(b, some)
        for r in range(3):
            gathered[0, piece, me, at, r : r + 1, :] = pos_ref[r : r + 1, cols]
            gathered[0, piece, me, at, 3 + r : 4 + r, :] = str_ref[r : r + 1, cols]

    after = jnp.where(g < slices - 2, spaces, jnp.where(g < slices - 1, 1, 0))
    pl.semaphore_wait(barrier, spaces - 1 + jnp.where(g > 0, after, 0))

    chips = spaces // 2
    tall = chips // 2
    core = lax.rem(me, 2)
    column = lax.rem(me // 2, 2)
    row = me // 4
    partner = me + 1 - 2 * core

    def twin(d, sign):
        other_column = lax.rem(column + d % 2, 2)
        other_row = lax.rem(row + tall + sign * (d // 2), tall)
        return 2 * (2 * other_row + other_column) + core

    def copy(slot, t, what, where, sem):
        return pltpu.make_async_remote_copy(
            src_ref=gathered.at[slot, t, what],
            dst_ref=gathered.at[slot, t, what],
            send_sem=send_sem.at[slot, t, sem],
            recv_sem=recv_sem.at[slot, t, what],
            device_id={"space": where},
            device_id_type=MESH,
        )

    order = sorted(range(1, chips), key=lambda d: (-(d % 2) - (d // 2), d))

    def mirror(p):
        return p + 1 - 2 * core

    def sends(slot, t):
        found = []
        for d in order:
            found.append(copy(slot, t, me, twin(d, 1), d))
            found.append(copy(slot, t, me, mirror(twin(d, 1)), chips + d))
        return found + [copy(slot, t, me, partner, 0)]

    def pass_copy(t, what, d):
        return pltpu.make_async_remote_copy(
            src_ref=outgoing.at[t],
            dst_ref=arriving.at[t, what],
            send_sem=give_sem.at[t, d],
            recv_sem=take_sem.at[t, what],
            device_id={"space": lax.rem(me + d, spaces), "tm": lax.rem(g + 1, slices)},
            device_id_type=MESH,
        )

    at_row = lax.broadcasted_iota(jnp.int32, (SUB, BLOCK), 0)

    def stack(values):
        found = values[0]
        for r, v in enumerate(values[1:]):
            found = jnp.where(at_row > r, v, found)
        return found

    def spread(v):
        return jnp.broadcast_to(v, (SUB, BLOCK))

    def source_block(tile, t, p, b, centre):
        rows = [tile[b, r : r + 1, :] for r in range(6)]
        x = [spread(v) - c for v, c in zip(rows[:3], centre)]
        a = [spread(v) for v in rows[3:]]
        square = dot3(x, x)
        six = a + cross(x, a)
        whole = stack([x[0], x[1], x[2], square, jnp.ones_like(square), x[0], x[1], x[2]])
        high, middle, low = split3(whole)
        second = jnp.where((at_row <= 2) | (at_row == 4), high, middle)
        third = jnp.where(at_row == 4, high, jnp.where(at_row <= 2, middle, low))
        at = p * blocks + t * some + b
        feat[at] = jnp.concatenate(
            [high, second, third, jnp.zeros_like(high)], 0
        ).astype(jnp.bfloat16)
        common = stack(six)
        inner = at_row <= 5
        parts = []
        for k in range(3):
            ends = jnp.where(at_row == 6, six[2 * k], six[2 * k + 1])
            parts.append(jnp.where(inner, common * x[k], ends))
        parts.append(common * square)
        pieces = split3(jnp.concatenate(parts, 0))
        moment[at] = jnp.concatenate(pieces, 0).astype(jnp.bfloat16)

    def source_features(tile, t, p, centre):
        for b in range(some):
            source_block(tile, t, p, b, centre)

    def target_features(t, centre):
        for b in range(some):
            x = [spread(mine[t, b, r : r + 1, :]) - centre[r] for r in range(3)]
            square = dot3(x, x) + core_square
            minus = [-2.0 * v for v in x]
            high, middle, low = split3(
                stack(minus + [jnp.ones_like(square), square] + minus)
            )
            first = jnp.where(at_row <= 4, high, middle)
            exact = (at_row == 3) | (at_row >= 5)
            second = jnp.where(exact, high, jnp.where(at_row == 4, middle, low))
            third = jnp.where(exact, high, jnp.where(at_row == 4, low, middle))
            rows = jnp.concatenate([first, second, third, jnp.zeros_like(first)], 0)
            coef[t * some + b] = rows.T.astype(jnp.bfloat16)

    group = 4 if width % 4 == 0 else 1

    def pair_product(i, j):
        at = [slot_ref[list_ref[i, j + k]] for k in range(group)]
        right = jnp.concatenate([feat[p] for p in at], 1)
        both = lax.dot_general(
            coef[i], right, (((1,), (0,)), ((), ())), preferred_element_type=jnp.float32
        )
        return at, both

    def pair_sums(at, both):
        inverse = lax.rsqrt(both)
        square = inverse * inverse
        weight = (square * square) * inverse
        high = weight.astype(jnp.bfloat16)
        low = (weight - high.astype(jnp.float32)).astype(jnp.bfloat16)
        moments = jnp.concatenate([moment[p] for p in at], 1)
        rows = (((1,), (1,)), ((), ()))
        return lax.dot_general(
            moments, high, rows, preferred_element_type=jnp.float32
        ) + lax.dot_general(moments, low, rows, preferred_element_type=jnp.float32)

    def some_targets(chosen, finish):
        work = [(n, j) for n in range(len(chosen) * some) for j in range(0, width, group)]
        waiting = []
        total = 0.0
        for k in range(len(work) + AHEAD):
            if k < len(work):
                n, j = work[k]
                waiting.append((n, pair_product(chosen[n // some] * some + n % some, j)))
            if k >= AHEAD:
                n, (at, both) = waiting.pop(0)
                total += pair_sums(at, both)
                if k - AHEAD == len(work) - 1 or work[k - AHEAD + 1][0] != n:
                    sums[n * TERMS : (n + 1) * TERMS, :] = (
                        total[2 * TERMS :] + total[TERMS : 2 * TERMS] + total[:TERMS]
                    )
                    total = 0.0
                    if (n + 1) % some == 0:
                        finish(n // some, chosen[n // some])

    def rates(u, t, centre):
        row = lambda r: jnp.concatenate([mine[t, b, r : r + 1, :] for b in range(some)], 0)
        x = [row(r) - centre[r] for r in range(3)]
        a = [row(3 + r) for r in range(3)]
        pick = lambda r: sums[pl.ds(u * some * TERMS + r, some, stride=TERMS), :]
        plain = [pick(SUB * (c // 2) + 6 + c % 2) for c in range(6)]
        along = [[pick(SUB * k + c) for c in range(6)] for k in range(3)]
        squared = [pick(SUB * 3 + c) for c in range(6)]
        near = dot3(x, x) + core_square
        turn = dot3(a, x)
        three = [
            near * plain[c] - 2.0 * dot3(x, [along[k][c] for k in range(3)]) + squared[c]
            for c in range(6)
        ]
        five = [
            turn * plain[c] - dot3(a, [along[k][c] for k in range(3)]) for c in range(6)
        ]
        cross_v = cross(x, three[:3])
        cross_s = cross(a, three[:3])
        cross_f = cross(x, five[:3])
        velocity = [-inv_four_pi * (cross_v[r] - three[3 + r]) for r in range(3)]
        stretch = [
            -inv_four_pi * (cross_s[r] - 3.0 * (cross_f[r] - five[3 + r])) for r in range(3)
        ]
        for r, v in enumerate(velocity + stretch):
            for b in range(some):
                rate[u, b, r : r + 1, :] = v[b : b + 1, :]

    second = 3 + g
    steps = jnp.where(g == 0, 4, jnp.where(g < slices - 1, g + 8, g + 7))

    for t in range(pieces):
        for each in sends(0, t):
            each.start()

    def step(s, carry):
        slot = lax.rem(s, 2)
        other = 1 - slot
        part = jnp.where(s < 4, s, s - second)
        joins = (part == 4) & (g > 1)
        own = list(range(pieces))
        for t in own:
            mine[t] = gathered[slot, t, me]

        @pl.when(joins)
        def _():
            pass_copy(last, me, 0).wait_recv()
            mine[last] = mine[last] + arriving[last, me]
            final[last] = mine[last]

        centre = []
        for r in range(3):
            every = sum(mine[t, b, r : r + 1, :] for t in own for b in range(some))
            centre.append(
                jnp.sum(every, keepdims=True) * (1.0 / (len(own) * some * BLOCK))
            )
        for t in own:
            target_features(t, centre)
            source_features(mine.at[t], t, me, centre)
        near = order[::-1]
        found = [partner]
        for d in near:
            found += [twin(d, -1), mirror(twin(d, -1))]
        for t in range(pieces):
            for p in found:
                copy(slot, t, p, p, 0).wait_recv()
                if t == last:

                    @pl.when(joins)
                    def _():
                        pass_copy(t, p, 0).wait_recv()
                        gathered[slot, t, p] = gathered[slot, t, p] + arriving[t, p]

                source_features(gathered.at[slot, t, p], t, p, centre)

        def finish(u, t):
            rates(u, t, centre)
            now = rate[u]
            current = mine[t]

            def put(value):
                gathered[other, t, me] = value

            @pl.when(part == 0)
            def _():
                base[t] = current
                f0[t] = now
                put(current + (0.5 * h) * now)

            @pl.when(part == 1)
            def _():
                f1[t] = now
                put(current + (0.5 * h) * now)

            @pl.when(part == 2)
            def _():
                f2[t] = now
                put(
                    base[t]
                    + h * (5.0 / 24.0 * f0[t] + 1.0 / 3.0 * f1[t] - 1.0 / 24.0 * now)
                )

            @pl.when(part == 3)
            def _():
                coarse = base[t] + h * f0[t]
                correction = (
                    current
                    + (0.5 * h) * (now - f1[t])
                    + h * (-1.0 / 24.0 * f0[t] + 1.0 / 3.0 * f1[t] + 5.0 / 24.0 * f2[t])
                    - coarse
                )

                @pl.when(s == 3)
                def _():
                    c0[t] = correction

                @pl.when((s > 3) & (g > 1) & (g < slices - 1))
                def _():
                    put(correction)

                @pl.when((s > 3) & (g > 1) & (g == slices - 1))
                def _():
                    final[t] = correction
                    if t == last:
                        for each in range(pieces):
                            pass_copy(each, me, 0).wait_recv()
                            final[each] = final[each] + arriving[each, me]

                @pl.when((s == 3) | (g <= 1))
                def _():
                    put(coarse + correction)
                    final[t] = coarse + correction

            @pl.when(part < 0)
            def _():
                put(current + h * now + c0[t])

            @pl.when(part == 4)
            def _():
                outgoing[t] = current + h * now
                pass_copy(t, me, 0).start()

                if t == last:

                    @pl.when(g < slices - 2)
                    def _():
                        for d in range(1, spaces):
                            pass_copy(t, me, d).start()

            meets = (part == 3) & (s > 3) & (g > 1)
            send_now = (s < steps - 1) if t == last else (s < steps - 1) & jnp.logical_not(meets)

            @pl.when(send_now)
            def _():
                for each in sends(other, t):
                    each.start()

            if t == last:

                @pl.when(meets & (s < steps - 1))
                def _():
                    for early in range(last):
                        pass_copy(early, me, 0).wait_recv()
                        value = gathered[other, early, me] + arriving[early, me]
                        gathered[other, early, me] = value
                        final[early] = value
                        for each in sends(other, early):
                            each.start()

        some_targets(list(range(pieces)), finish)
        for t in range(pieces):
            for each in sends(slot, t):
                each.wait_send()
        return carry

    lax.fori_loop(0, steps, step, 0)

    for t in range(pieces):
        for b in range(some):
            for r in range(6):
                at = r * blocks + t * some + b
                out_ref[at : at + 1, :] = final[t, b, r : r + 1, :]

    @pl.when((g > 0) & (g < slices - 1))
    def _():
        for t in range(pieces):
            pass_copy(t, me, 0).wait_send()

    @pl.when((g > 0) & (g < slices - 2))
    def _():
        for d in range(1, spaces):
            pass_copy(last, me, d).wait_send()


def per_device(spaces, slices, positions, strengths, source_lists, block_slot):
    blocks, width = source_lists.shape
    whole = block_slot.shape[0]
    pieces = 2 if blocks % 2 == 0 else 1
    tiles = (blocks // pieces, 6, BLOCK)
    state = pltpu.VMEM((pieces,) + tiles, jnp.float32)
    anywhere = pl.BlockSpec(memory_space=pl.ANY)
    out = pl.pallas_call(
        functools.partial(kernel, spaces, slices, blocks, width, pieces),
        out_shape=jax.ShapeDtypeStruct((6 * blocks, BLOCK), jnp.float32),
        in_specs=[anywhere] * 4,
        out_specs=pl.BlockSpec(memory_space=pltpu.VMEM),
        scratch_shapes=[
            pltpu.VMEM(positions.shape, jnp.float32),
            pltpu.VMEM(strengths.shape, jnp.float32),
            pltpu.SMEM(source_lists.shape, jnp.int32),
            pltpu.SMEM(block_slot.shape, jnp.int32),
            pltpu.VMEM((2, pieces, spaces) + tiles, jnp.float32),
            state,
            pltpu.VMEM((pieces,) + tiles, jnp.float32),
            state, state, state, state, state, state,
            pltpu.VMEM((pieces, spaces) + tiles, jnp.float32),
            state,
            pltpu.VMEM((blocks * TERMS, BLOCK), jnp.float32),
            pltpu.VMEM((whole, DEPTH, BLOCK), jnp.bfloat16),
            pltpu.VMEM((whole, PIECES * TERMS, BLOCK), jnp.bfloat16),
            pltpu.VMEM((blocks, BLOCK, DEPTH), jnp.bfloat16),
            pltpu.SemaphoreType.DMA((4,)),
            pltpu.SemaphoreType.DMA((2, pieces, spaces)),
            pltpu.SemaphoreType.DMA((2, pieces, spaces)),
            pltpu.SemaphoreType.DMA((pieces, spaces)),
            pltpu.SemaphoreType.DMA((pieces, spaces)),
        ],
        compiler_params=pltpu.CompilerParams(collective_id=0, has_side_effects=True),
    )(positions, strengths, source_lists, block_slot)
    return out.reshape(1, 6, blocks * BLOCK)


def solution(mesh):
    return jax.shard_map(
        functools.partial(per_device, mesh.shape["space"], mesh.shape["tm"]),
        mesh=mesh,
        in_specs=(P(None, "space"), P(None, "space"), P("space", None), P()),
        out_specs=P("tm", None, "space"),
        check_vma=False,
    )
```
